32 devices in a mesh: img: 8 (over z, y), seq: 4 (over x, core).
Axes of the slice: x: 2, y: 2, z: 4, core: 2. Of those that a mesh axis runs over, the one named last changes fastest.
Arguments:
- tokens: bfloat16 [8192, 1152], P(('img', 'seq')), may hold values from -6 to 6
- conditioning: float32 [32, 1152], P('img'), may hold values from -6 to 6
- slot_ids: int32 [8192], P('img'), may hold values from 0 to 3, as said below
- dino_target: bfloat16 [8192, 768], P(('img', 'seq')), may hold values from -6 to 6
- out_cotangent: bfloat16 [8192, 1152], P(('img', 'seq')), may hold values from -6 to 6
- ada_weight: bfloat16 [1152, 6912], P('img', 'seq'), may hold values from -0.1875 to 0.1875
- qkv_weight: bfloat16 [1152, 3456], P('img', 'seq'), may hold values from -0.1875 to 0.1875
- attn_weight: bfloat16 [1152, 1152], P('img', 'seq'), may hold values from -0.75 to 0.75
- up_weight: bfloat16 [1152, 4608], P('img', 'seq'), may hold values from -0.1875 to 0.1875
- down_weight: bfloat16 [4608, 1152], P('img', 'seq'), may hold values from -0.09375 to 0.09375
- first_proj: bfloat16 [1152, 2048], P('img', 'seq'), may hold values from -0.1875 to 0.1875
- second_proj: bfloat16 [2048, 2048], P('img', 'seq'), may hold values from -0.125 to 0.125
- third_proj: bfloat16 [2048, 768], P('img', 'seq'), may hold values from -0.125 to 0.125
- ada_bias: float32 [6912], replicated, may hold values from -2 to 2
- query_bias: float32 [1152], replicated, may hold values from -2 to 2
- value_bias: float32 [1152], replicated, may hold values from -2 to 2
- attn_bias: float32 [1152], replicated, may hold values from -2 to 2
- up_bias: float32 [4608], replicated, may hold values from -2 to 2
- down_bias: float32 [1152], replicated, may hold values from -2 to 2
- first_bias: float32 [2048], replicated, may hold values from -2 to 2
- second_bias: float32 [2048], replicated, may hold values from -2 to 2
- third_bias: float32 [768], replicated, may hold values from -2 to 2
Outputs:
- block_output: bfloat16 [8192, 1152], P(('img', 'seq'))
- tokens_grad: float32 [8192, 1152], P(('img', 'seq'))
- conditioning_grad: float32 [32, 1152], P('img')
- ada_weight_grad: float32 [1152, 6912], P('img', 'seq')
- qkv_weight_grad: float32 [1152, 3456], P('img', 'seq')
- attn_weight_grad: float32 [1152, 1152], P('img', 'seq')
- up_weight_grad: float32 [1152, 4608], P('img', 'seq')
- down_weight_grad: float32 [4608, 1152], P('img', 'seq')
- first_proj_grad: float32 [1152, 2048], P('img', 'seq')
- second_proj_grad: float32 [2048, 2048], P('img', 'seq')
- third_proj_grad: float32 [2048, 768], P('img', 'seq')
- ada_bias_grad: float32 [6912], replicated
- query_bias_grad: float32 [1152], replicated
- value_bias_grad: float32 [1152], replicated
- attn_bias_grad: float32 [1152], replicated
- up_bias_grad: float32 [4608], replicated
- down_bias_grad: float32 [1152], replicated
- first_bias_grad: float32 [2048], replicated
- second_bias_grad: float32 [2048], replicated
- third_bias_grad: float32 [768], replicated
The draws below stay inside these ranges and needn't reach their ends.
Inputs may be any that keep to these rules, and one draw needn't show every extreme that they name: `slot_ids`: within each group of 1024 consecutive tokens the values start at 0 and never fall; each value covers 256 or 1024 consecutive tokens beginning at a multiple of 256 from the group's start.
All inputs are finite; a program needn't handle non-finite values.
Results may differ from the reference program's by a relative error of at most 0.019.
Values may be sent and summed in bfloat16 or wider, within the bound.
No kernel may reach another device: no remote copies, remote signals or barrier semaphores. Data moves between devices by JAX's collectives and lax.ppermute only.
A program may use at most 320 MiB of HBM per device.

```python
from functools import partial
import jax
import jax.numpy as jnp
from jax import lax

D = 1152
H = 16
HD = 72
FF = 4608
PH = 2048
ZD = 768
SHORT = 256
LONG = 1024
TOK_GRP = 1024
SLOTS = 4
IMAGE_SLOTS = 32
TOKENS = 8192


def draw_slot_ids(key, part):
    groups = TOKENS // TOK_GRP
    unit_count = TOK_GRP // SHORT
    long_ratio = LONG // SHORT
    most_long = unit_count // long_ratio
    count_key = jax.random.fold_in(key, 11)
    order_key = jax.random.fold_in(key, 23)
    long_count = jax.random.randint(count_key, (groups,), 0, most_long + 1)
    long_count = long_count.at[0].set(0).at[groups - 1].set(most_long)
    positions = jnp.arange(unit_count, dtype=jnp.int32)
    item_count = unit_count - (long_ratio - 1) * long_count
    is_long = positions[None, :] < long_count[:, None]
    is_valid = positions[None, :] < item_count[:, None]
    item_scores = jax.random.randint(order_key, (groups, unit_count), 0, 1 << 20) * unit_count + positions[None, :]
    item_scores = jnp.where(is_valid, item_scores, (1 << 30) + positions[None, :])
    ordering = jnp.argsort(item_scores, axis=1, stable=True)
    long_sorted = jnp.take_along_axis(is_long, ordering, axis=1)
    valid_sorted = jnp.take_along_axis(is_valid, ordering, axis=1)
    item_size = jnp.where(valid_sorted, jnp.where(long_sorted, long_ratio, 1), 0)
    item_start = jnp.cumsum(item_size, axis=1) - item_size
    started = valid_sorted[:, None, :] & (item_start[:, None, :] <= positions[None, :, None])
    unit_slot = jnp.sum(started.astype(jnp.int32), axis=2) - 1
    return jnp.repeat(unit_slot, SHORT, axis=1).reshape(groups * TOK_GRP).astype(jnp.int32)


def levels(stream_key, shape, shards, low, top_value):
    gain, own = 1.0, jax.random.fold_in(stream_key, 6)
    for position, parts in shards:
        draws = jnp.exp(jax.random.uniform(jax.random.fold_in(own, position), (parts,), jnp.float32, low / len(shards), top_value / len(shards)))
        gain = gain * jnp.repeat(draws, shape[position] // parts).reshape([-1 if axis == position else 1 for axis in range(len(shape))])
    return gain


def bell_draw(own_key, dims, scale, bound, shards=(), kind=jnp.bfloat16):
    gain = levels(own_key, dims, shards, -0.22, 0.18) if shards else 1.0
    array = jax.random.normal(own_key, dims, jnp.float32) * scale * gain
    return jnp.minimum(jnp.maximum(array, -bound), bound).astype(kind)


def setup_inputs(seed: int = 0) -> dict:
    key_list = jax.random.split(jax.random.key(seed), 23)
    tokens = bell_draw(key_list[0], (TOKENS, D), 1.0, 6.0, ((0, 32),))
    conditioning = bell_draw(key_list[1], (IMAGE_SLOTS, D), 1.0, 6.0, ((0, 8),), jnp.float32)
    slot_ids = draw_slot_ids(jax.random.fold_in(key_list[22], 71), 0)
    dino_target = bell_draw(key_list[3], (TOKENS, ZD), 1.0, 6.0, ((0, 32),))
    out_cotangent = bell_draw(key_list[4], (TOKENS, D), 1.0, 6.0, ((0, 32),))
    ada_weight = bell_draw(key_list[5], (D, 6 * D), D ** -0.5, 0.1875, ((0, 8), (1, 4)))
    qkv_weight = bell_draw(key_list[6], (D, 3 * D), D ** -0.5, 0.1875, ((0, 8), (1, 4)))
    attn_weight = bell_draw(key_list[7], (D, D), (D // 16) ** -0.5, 0.75, ((0, 8), (1, 4)))
    up_weight = bell_draw(key_list[8], (D, FF), D ** -0.5, 0.1875, ((0, 8), (1, 4)))
    down_weight = bell_draw(key_list[9], (FF, D), FF ** -0.5, 0.09375, ((0, 8), (1, 4)))
    first_proj = bell_draw(key_list[10], (D, PH), D ** -0.5, 0.1875, ((0, 8), (1, 4)))
    second_proj = bell_draw(key_list[11], (PH, PH), PH ** -0.5, 0.125, ((0, 8), (1, 4)))
    third_proj = bell_draw(key_list[12], (PH, ZD), PH ** -0.5, 0.125, ((0, 8), (1, 4)))
    ada_bias = bell_draw(key_list[13], (6 * D,), 0.3, 2.0, (), jnp.float32)
    query_bias = bell_draw(key_list[14], (D,), 0.3, 2.0, (), jnp.float32)
    value_bias = bell_draw(key_list[15], (D,), 0.3, 2.0, (), jnp.float32)
    attn_bias = bell_draw(key_list[16], (D,), 0.3, 2.0, (), jnp.float32)
    up_bias = bell_draw(key_list[17], (FF,), 0.3, 2.0, (), jnp.float32)
    down_bias = bell_draw(key_list[18], (D,), 0.3, 2.0, (), jnp.float32)
    first_bias = bell_draw(key_list[19], (PH,), 0.3, 2.0, (), jnp.float32)
    second_bias = bell_draw(key_list[20], (PH,), 0.3, 2.0, (), jnp.float32)
    third_bias = bell_draw(key_list[21], (ZD,), 0.3, 2.0, (), jnp.float32)
    return {"tokens": tokens, "conditioning": conditioning, "slot_ids": slot_ids, "dino_target": dino_target, "out_cotangent": out_cotangent, "ada_weight": ada_weight, "qkv_weight": qkv_weight, "attn_weight": attn_weight, "up_weight": up_weight, "down_weight": down_weight, "first_proj": first_proj, "second_proj": second_proj, "third_proj": third_proj, "ada_bias": ada_bias, "query_bias": query_bias, "value_bias": value_bias, "attn_bias": attn_bias, "up_bias": up_bias, "down_bias": down_bias, "first_bias": first_bias, "second_bias": second_bias, "third_bias": third_bias}


@jax.custom_vjp
def low(v):
    return lax.optimization_barrier(v.astype(jnp.bfloat16)).astype(jnp.float32)

@jax.custom_vjp
def low_back(v):
    return v

def low_keep(v):
    return (low(v), None)

def low_pass(kept, grad):
    return (grad,)

def back_keep(v):
    return (v, None)

def back_low(kept, grad):
    return (low(grad),)
low.defvjp(low_keep, low_pass)
low_back.defvjp(back_keep, back_low)
EPS_NORM = 1e-06
EPS_COS = 1e-06
LAMBDA_ALIGN = 0.5
MASKED_SCORE = -1e+30
HIGHEST_PREC = lax.Precision.HIGHEST

def product(left, right):
    return jnp.dot(left, right, precision=HIGHEST_PREC, preferred_element_type=jnp.float32)

def layer_norm(values):
    centered = values - lax.optimization_barrier(jnp.mean(values, axis=-1, keepdims=True))
    return centered * lax.rsqrt(lax.optimization_barrier(jnp.mean(centered * centered, axis=-1, keepdims=True)) + EPS_NORM)

def cosine_total(aligned, target):
    cosine = lax.optimization_barrier(jnp.sum(aligned * target, axis=1)) * lax.rsqrt(lax.optimization_barrier(jnp.sum(aligned * aligned, axis=1)) + EPS_COS) * lax.rsqrt(lax.optimization_barrier(jnp.sum(target * target, axis=1)) + EPS_COS)
    return -LAMBDA_ALIGN * jnp.sum(cosine)

def head_attention(same_image, pieces):
    queries, key_rows, value_rows = pieces
    scores = low_back(product(queries, key_rows.T) * HD ** (-0.5))
    scores = jnp.where(same_image, scores, MASKED_SCORE)
    weights = low(jax.nn.softmax(scores, axis=-1))
    return product(weights, value_rows)

def to_heads(matrix):
    return matrix.reshape(TOK_GRP, H, HD).transpose(1, 0, 2)

def group_layer(params, group):
    qkv_w, attn_w, up_w, down_w, first_w, second_w, third_w, query_b, value_b, attn_b, up_b, down_b, first_b, second_b, third_b = params
    tokens_f, group_slots, target, group_mod = group
    mod_rows = jnp.take(group_mod, group_slots, axis=0)
    shift_a, scale_a, gate_a, shift_b, scale_b, gate_b = jnp.split(mod_rows, 6, axis=1)
    hidden_a = low(layer_norm(tokens_f) * (1.0 + scale_a) + shift_a)
    qkv_rows = product(hidden_a, qkv_w)
    queries = low(low_back(qkv_rows[:, :D] + query_b))
    key_rows = low(low_back(qkv_rows[:, D:2 * D]))
    value_rows = low(low_back(qkv_rows[:, 2 * D:] + value_b))
    same_image = group_slots[:, None] == group_slots[None, :]
    attended = lax.map(jax.checkpoint(partial(head_attention, same_image)), (to_heads(queries), to_heads(key_rows), to_heads(value_rows)))
    attended = low(low_back(attended.transpose(1, 0, 2).reshape(TOK_GRP, D)))
    branch_a = low_back(product(attended, attn_w) + attn_b)
    after_attn = tokens_f + gate_a * branch_a
    hidden_b = low(layer_norm(after_attn) * (1.0 + scale_b) + shift_b)
    pre_act = low_back(product(hidden_b, up_w) + up_b)
    activation = low(jax.nn.gelu(pre_act, approximate=True))
    branch_b = low_back(product(activation, down_w) + down_b)
    result = after_attn + gate_b * branch_b
    feed_low = low(result)
    first_act = low(jax.nn.silu(low_back(product(feed_low, first_w) + first_b)))
    second_act = low(jax.nn.silu(low_back(product(first_act, second_w) + second_b)))
    aligned = low_back(product(second_act, third_w) + third_b)
    return (result, cosine_total(aligned, target))

def reference(tokens, conditioning, slot_ids, dino_target, out_cotangent, ada_weight, qkv_weight, attn_weight, up_weight, down_weight, first_proj, second_proj, third_proj, ada_bias, query_bias, value_bias, attn_bias, up_bias, down_bias, first_bias, second_bias, third_bias):
    groups = TOKENS // TOK_GRP
    target_groups = dino_target.astype(jnp.float32).reshape(groups, TOK_GRP, ZD)
    slot_groups = slot_ids.reshape(groups, TOK_GRP)
    params = (qkv_weight.astype(jnp.float32), attn_weight.astype(jnp.float32), up_weight.astype(jnp.float32), down_weight.astype(jnp.float32), first_proj.astype(jnp.float32), second_proj.astype(jnp.float32), third_proj.astype(jnp.float32), query_bias, value_bias, attn_bias, up_bias, down_bias, first_bias, second_bias, third_bias)

    def forward(tokens_f, cond_f, ada_w, ada_b, layer_params):
        cond_act = low(jax.nn.silu(cond_f))
        modulation = low_back(product(cond_act, ada_w) + ada_b).reshape(groups, SLOTS, 6 * D)
        step_layer = jax.checkpoint(partial(group_layer, layer_params))

        def scan_step(running, group):
            result, align = step_layer(group)
            return (running + align, result)
        running, results = lax.scan(scan_step, jnp.zeros((), jnp.float32), (tokens_f.reshape(groups, TOK_GRP, D), slot_groups, target_groups, modulation))
        return (results.reshape(TOKENS, D), running)
    primal, pullback = jax.vjp(forward, tokens.astype(jnp.float32), conditioning, ada_weight.astype(jnp.float32), ada_bias, params)
    results, running = primal
    tokens_grad, cond_grad, ada_grad, ada_bias_grad, layer_grads = pullback((out_cotangent.astype(jnp.float32), jnp.ones_like(running)))
    return (results.astype(jnp.bfloat16), tokens_grad, cond_grad, ada_grad, layer_grads[0], layer_grads[1], layer_grads[2], layer_grads[3], layer_grads[4], layer_grads[5], layer_grads[6], ada_bias_grad, layer_grads[7], layer_grads[8], layer_grads[9], layer_grads[10], layer_grads[11], layer_grads[12], layer_grads[13], layer_grads[14])
```

```python
import jax
import jax.numpy as jnp
from jax import lax
from jax.experimental import pallas as pl
from jax.experimental.pallas import tpu as pltpu
from jax.sharding import PartitionSpec as P

H = 16
HD = 72
LANES = 128
EPS_NORM = 1e-06
EPS_COS = 1e-06
LAMBDA_ALIGN = 0.5
MASKED_SCORE = -1e30
F32 = jnp.float32
BF16 = jnp.bfloat16
SEQ = 4


def product(left, right, out=F32):
    return lax.dot_general(
        left, right, (((1,), (0,)), ((), ())), preferred_element_type=F32
    ).astype(out)


def product_tn(left, right, out=F32):
    return lax.dot_general(
        left, right, (((0,), (0,)), ((), ())), preferred_element_type=F32
    ).astype(out)


def product_nt(left, right, out=F32):
    return lax.dot_general(
        left, right, (((1,), (1,)), ((), ())), preferred_element_type=F32
    ).astype(out)


def column_sums(values):
    return jnp.sum(values.astype(F32), axis=0)


def norm_parts(values):
    centered = values - jnp.mean(values, axis=-1, keepdims=True)
    inverse = lax.rsqrt(jnp.mean(centered * centered, axis=-1, keepdims=True) + EPS_NORM)
    return centered * inverse, inverse


def norm_back(normed, inverse, grad):
    return inverse * (
        grad
        - jnp.mean(grad, axis=-1, keepdims=True)
        - normed * jnp.mean(grad * normed, axis=-1, keepdims=True)
    )


def silu_parts(values):
    gate = 1.0 / (1.0 + jnp.exp(-values))
    return values * gate, gate * (1.0 + values * (1.0 - gate))


GELU_C = 0.7978845608028654


def gelu_parts(values):
    inner = GELU_C * (values + 0.044715 * values * values * values)
    bent = jnp.tanh(inner)
    slope = GELU_C * (1.0 + 3.0 * 0.044715 * values * values)
    value = 0.5 * values * (1.0 + bent)
    return value, 0.5 * (1.0 + bent) + 0.5 * values * (1.0 - bent * bent) * slope


def swap(values, distance):
    return lax.ppermute(values, "seq", [(i, i ^ distance) for i in range(SEQ)])


def gather_rows(own):
    across = swap(own, 2)
    near = swap(own, 1)
    far = swap(across, 1)
    return jnp.concatenate([own, near], 0), jnp.concatenate([across, far], 0)


def scatter_rows(near, far):
    rows = near.shape[0] // 2
    from_far = swap(far[rows:], 1)
    across = swap((far[:rows].astype(F32) + from_far.astype(F32)).astype(BF16), 2)
    from_near = swap(near[rows:], 1)
    return near[:rows].astype(F32) + from_near.astype(F32) + across.astype(F32)


def img_swap(values):
    count = lax.axis_size("img")
    return lax.ppermute(values, "img", [(i, i ^ 1) for i in range(count)])


def slow_groups():
    half = lax.axis_size("img") // 2
    return [[2 * k + fast for k in range(half)] for fast in range(2)]


def gather_img(shard):
    half = lax.axis_size("img") // 2
    fast = lax.axis_index("img") % 2
    copies = jnp.broadcast_to(shard[None], (half,) + shard.shape)
    mine = lax.all_to_all(
        copies, "img", split_axis=0, concat_axis=0, tiled=True, axis_index_groups=slow_groups()
    )
    other = img_swap(mine)
    return mine, other, fast


def interleave(gathered, first, count):
    mine, other, fast = gathered
    half, rows = mine.shape[:2]
    mine, other = mine[:, :, first : first + count], other[:, :, first : first + count]
    even = jnp.where(fast == 0, mine, other)
    odd = jnp.where(fast == 0, other, mine)
    return jnp.concatenate([even[:, None], odd[:, None]], 1).reshape(2 * half * rows, count)


def reduce_img(blocks):
    count, rows, cols = blocks.shape
    half = count // 2
    fast = lax.axis_index("img") % 2
    pairs = blocks.reshape(half, 2, rows, cols)
    keep = jnp.where(fast == 0, pairs[:, 0], pairs[:, 1])
    send = jnp.where(fast == 0, pairs[:, 1], pairs[:, 0])
    joined = (keep.astype(F32) + img_swap(send).astype(F32)).astype(BF16)
    parts = lax.all_to_all(
        joined, "img", split_axis=0, concat_axis=0, tiled=True, axis_index_groups=slow_groups()
    )
    return jnp.sum(parts.astype(F32), axis=0)


def seq_exchange(parts):
    return lax.all_to_all(parts, "seq", split_axis=0, concat_axis=0, tiled=True)


def img_exchange(parts):
    return lax.all_to_all(parts, "img", split_axis=0, concat_axis=0, tiled=True)


def img_gather(values):
    count = lax.axis_size("img")
    return img_exchange(jnp.broadcast_to(values[None], (count,) + values.shape))


def pick(stacked, index):
    return lax.dynamic_index_in_dim(stacked, index, 0, keepdims=False)


def attend_kernel(slots, q_ref, k_ref, v_ref, out_ref):
    rows = q_ref.shape[0] // SEQ
    scale = HD ** (-0.5)
    keys = k_ref[...]
    values = v_ref[...]
    for block in range(SEQ):
        queries = q_ref[block * rows : (block + 1) * rows, :]
        scores = lax.dot_general(
            queries, keys, (((1,), (1,)), ((), ())), preferred_element_type=F32
        )
        scores = jnp.concatenate(
            [
                jnp.where(
                    slots[block] == slots[other],
                    scores[:, other * rows : (other + 1) * rows] * scale,
                    MASKED_SCORE,
                )
                for other in range(SEQ)
            ],
            axis=1,
        )
        raised = jnp.exp(scores - jnp.max(scores, axis=1, keepdims=True))
        probs = raised / jnp.sum(raised, axis=1, keepdims=True)
        out_ref[block * rows : (block + 1) * rows, :] = jnp.dot(
            probs.astype(BF16), values, preferred_element_type=F32
        ).astype(BF16)


def attend_back_kernel(slots, q_ref, k_ref, v_ref, g_ref, gq_ref, gk_ref, gv_ref, gk_sum, gv_sum):
    rows = q_ref.shape[0] // SEQ
    scale = HD ** (-0.5)
    keys = k_ref[...]
    values = v_ref[...]
    for block in range(SEQ):
        queries = q_ref[block * rows : (block + 1) * rows, :]
        grads = g_ref[block * rows : (block + 1) * rows, :]
        scores = lax.dot_general(
            queries, keys, (((1,), (1,)), ((), ())), preferred_element_type=F32
        )
        scores = jnp.concatenate(
            [
                jnp.where(
                    slots[block] == slots[other],
                    scores[:, other * rows : (other + 1) * rows] * scale,
                    MASKED_SCORE,
                )
                for other in range(SEQ)
            ],
            axis=1,
        )
        raised = jnp.exp(scores - jnp.max(scores, axis=1, keepdims=True))
        probs = raised / jnp.sum(raised, axis=1, keepdims=True)
        grad_probs = lax.dot_general(
            grads, values, (((1,), (1,)), ((), ())), preferred_element_type=F32
        )
        delta = jnp.sum(probs * grad_probs, axis=1, keepdims=True)
        grad_scores = (probs * (grad_probs - delta)).astype(BF16)
        gq_ref[block * rows : (block + 1) * rows, :] = (
            jnp.dot(grad_scores, keys, preferred_element_type=F32) * scale
        ).astype(BF16)
        gk = lax.dot_general(
            grad_scores, queries, (((0,), (0,)), ((), ())), preferred_element_type=F32
        )
        gv = lax.dot_general(
            probs.astype(BF16), grads, (((0,), (0,)), ((), ())), preferred_element_type=F32
        )
        if block == 0:
            gk_sum[...] = gk
            gv_sum[...] = gv
        else:
            gk_sum[...] += gk
            gv_sum[...] += gv
    gk_ref[...] = (gk_sum[...] * scale).astype(BF16)
    gv_ref[...] = gv_sum[...].astype(BF16)


def head_block(rows, first):
    return pl.BlockSpec((rows, LANES), lambda head, slots: (0, first + head))


def attend_forward(qkv, slots):
    rows, heads = qkv.shape[0], qkv.shape[1] // (3 * LANES)
    return pl.pallas_call(
        attend_kernel,
        grid_spec=pltpu.PrefetchScalarGridSpec(
            num_scalar_prefetch=1,
            grid=(heads,),
            in_specs=[head_block(rows, kind * heads) for kind in range(3)],
            out_specs=head_block(rows, 0),
        ),
        out_shape=jax.ShapeDtypeStruct((rows, heads * LANES), BF16),
        name="attend",
    )(slots, qkv, qkv, qkv)


def attend_backward(qkv, grads, slots):
    rows, heads = qkv.shape[0], qkv.shape[1] // (3 * LANES)
    shape = jax.ShapeDtypeStruct((rows, heads * LANES), BF16)
    return pl.pallas_call(
        attend_back_kernel,
        grid_spec=pltpu.PrefetchScalarGridSpec(
            num_scalar_prefetch=1,
            grid=(heads,),
            in_specs=[head_block(rows, kind * heads) for kind in range(3)] + [head_block(rows, 0)],
            out_specs=[head_block(rows, 0)] * 3,
            scratch_shapes=[pltpu.VMEM((rows, LANES), F32)] * 2,
        ),
        out_shape=(shape,) * 3,
        name="attend_back",
    )(slots, qkv, qkv, qkv, grads)


def pad_heads(values):
    lead = values.shape[:-1]
    heads = values.shape[-1] // HD
    parted = values.reshape(lead + (heads, HD))
    padded = jnp.pad(parted, [(0, 0)] * len(lead) + [(0, 0), (0, LANES - HD)])
    return padded.reshape(lead + (heads * LANES,))


def strip_heads(values):
    lead = values.shape[:-1]
    heads = values.shape[-1] // LANES
    return values.reshape(lead + (heads, LANES))[..., :HD].reshape(lead + (heads * HD,))


def local(
    tokens,
    conditioning,
    slot_ids,
    dino_target,
    out_cotangent,
    ada_weight,
    qkv_weight,
    attn_weight,
    up_weight,
    down_weight,
    first_proj,
    second_proj,
    third_proj,
    ada_bias,
    query_bias,
    value_bias,
    attn_bias,
    up_bias,
    down_bias,
    first_bias,
    second_bias,
    third_bias,
):
    own_rows, width = tokens.shape
    place = lax.axis_index("seq")
    img = lax.axis_size("img")
    slot_count = conditioning.shape[0]
    part_width = width // SEQ
    feat = qkv_weight.shape[0]
    mod_cols = ada_weight.shape[1]
    ff = up_bias.shape[0]
    ph = first_bias.shape[0]
    zd = third_bias.shape[0]
    ff_part = ff // SEQ
    ph_part = ph // SEQ
    ff_cell = ff // img // SEQ
    ph_cell = ph // img // SEQ

    dests = jnp.arange(SEQ, dtype=jnp.int32)
    three = qkv_weight.reshape(feat, 3, part_width).transpose(1, 0, 2)
    qkv_send = jnp.stack([pick(three, jnp.minimum((d - 3 * place) % SEQ, 2)) for d in range(SEQ)])
    qkv_got = seq_exchange(qkv_send)
    qkv_shard = jnp.concatenate(
        [pick(qkv_got, (kind * SEQ + place) // 3) for kind in range(3)], axis=1
    )
    qkv_all = gather_img(qkv_shard)

    rows_full = gather_rows(tokens)

    up_send = up_weight.reshape(feat, img // SEQ, SEQ, ff_cell).transpose(2, 0, 1, 3)
    up_send = up_send.reshape(SEQ, feat, part_width)
    down_send = down_weight.reshape(SEQ, ff_cell, part_width)
    first_send = first_proj.reshape(feat, img // SEQ, SEQ, ph_cell).transpose(2, 0, 1, 3)
    first_send = first_send.reshape(SEQ, feat, ph_part // SEQ)
    mlp_got = seq_exchange(jnp.concatenate([up_send, down_send, first_send], axis=2))
    second_got = seq_exchange(second_proj.reshape(SEQ, ph_cell, ph_part))
    mlp_got = mlp_got.transpose(1, 0, 2)
    up_shard = mlp_got[:, :, :part_width].reshape(feat, ff_part)
    down_shard = mlp_got[:, :, part_width : 2 * part_width].reshape(ff_cell, width)
    first_shard = mlp_got[:, :, 2 * part_width :].reshape(feat, ph_part)
    second_shard = second_got.transpose(1, 0, 2).reshape(ph_cell, ph)
    third_shard = third_proj.reshape(ph_cell, zd)

    cond_act, cond_slope = silu_parts(conditioning)
    cond_low = cond_act.astype(BF16)
    cond_cols = img_exchange(cond_low.reshape(slot_count, img, feat).transpose(1, 0, 2))
    cond_cols = cond_cols.reshape(img * slot_count, feat)
    mod_parts = img_exchange(product(cond_cols, ada_weight).reshape(img, slot_count, mod_cols))
    my_bias = lax.dynamic_slice_in_dim(ada_bias, place * mod_cols, mod_cols, 0)
    modulation = lax.all_gather(jnp.sum(mod_parts, axis=0) + my_bias, "seq", axis=1, tiled=True)
    block_slots = jnp.stack([slot_ids[(place ^ p) * own_rows] for p in range(SEQ)])
    block_mod = jnp.stack([pick(modulation, block_slots[p]) for p in range(SEQ)])
    shift_a, scale_a, gate_a, shift_b, scale_b, gate_b = jnp.split(block_mod[0], 6)

    def modulated(rows, first):
        normed, _ = norm_parts(rows.astype(F32).reshape(2, own_rows, width))
        shift = block_mod[first : first + 2, None, :width]
        scale = block_mod[first : first + 2, None, width : 2 * width]
        return (normed * (1.0 + scale) + shift).astype(BF16).reshape(2 * own_rows, width)

    hidden_a = jnp.concatenate([modulated(rows_full[0], 0), modulated(rows_full[1], 2)], 0)
    qkv_w = pad_heads(interleave(qkv_all, 0, 3 * part_width))
    q_bias = lax.dynamic_slice_in_dim(query_bias, place * part_width, part_width, 0)
    v_bias = lax.dynamic_slice_in_dim(value_bias, place * part_width, part_width, 0)
    qkv_bias = pad_heads(jnp.concatenate([q_bias, jnp.zeros_like(q_bias), v_bias]))
    qkv = (product(hidden_a, qkv_w) + qkv_bias).astype(BF16)
    attended_h = attend_forward(qkv, block_slots)
    attended_h = strip_heads(attended_h).reshape(SEQ, own_rows, part_width)
    heads_rel = jnp.stack([attended_h[0]] + [swap(attended_h[p], p) for p in range(1, SEQ)])
    attended = jnp.concatenate([pick(heads_rel, place ^ j) for j in range(SEQ)], axis=1)

    attn_up = gather_img(jnp.concatenate([attn_weight, up_shard], axis=1))
    attn_w = lax.all_gather(interleave(attn_up, 0, part_width), "seq", axis=1, tiled=True)
    up_w = interleave(attn_up, part_width, ff_part)
    down_first = gather_img(jnp.concatenate([down_shard, first_shard], axis=1))
    down_w = interleave(down_first, 0, width)
    first_w = interleave(down_first, width, ph_part)
    second_third = gather_img(jnp.concatenate([second_shard, third_shard], axis=1))
    second_w = interleave(second_third, 0, ph)
    third_w = interleave(second_third, ph, zd).reshape(ph, zd // SEQ)
    third_w = lax.all_gather(third_w, "seq", axis=1, tiled=True)

    tokens_f = tokens.astype(F32)
    branch_a = product(attended, attn_w) + attn_bias
    after_attn = tokens_f + gate_a * branch_a
    normed_b, inverse_b = norm_parts(after_attn)
    hidden_b = gather_rows((normed_b * (1.0 + scale_b) + shift_b).astype(BF16))

    my_up_bias = up_bias.reshape(img, SEQ, ff_cell)
    my_up_bias = lax.dynamic_index_in_dim(my_up_bias, place, 1, keepdims=False).reshape(ff_part)
    acts, slopes, sums = [], [], []
    for side in range(2):
        value, slope = gelu_parts(product(hidden_b[side], up_w) + my_up_bias)
        acts.append(value.astype(BF16))
        slopes.append(slope)
        sums.append(product(acts[side], down_w, BF16))
    branch_b = scatter_rows(*sums) + down_bias
    result = after_attn + gate_b * branch_b
    feed_low = result.astype(BF16)

    feed = gather_rows(feed_low)
    my_first_bias = first_bias.reshape(img, SEQ, ph_cell)
    my_first_bias = lax.dynamic_index_in_dim(my_first_bias, place, 1, keepdims=False)
    my_first_bias = my_first_bias.reshape(ph_part)
    first_acts, first_slopes, sums = [], [], []
    for side in range(2):
        value, slope = silu_parts(product(feed[side], first_w) + my_first_bias)
        first_acts.append(value.astype(BF16))
        first_slopes.append(slope)
        sums.append(product(first_acts[side], second_w, BF16))
    second_act, second_slope = silu_parts(scatter_rows(*sums) + second_bias)
    second_low = second_act.astype(BF16)
    aligned = product(second_low, third_w) + third_bias

    target = dino_target.astype(F32)
    inv_z = lax.rsqrt(jnp.sum(aligned * aligned, axis=1, keepdims=True) + EPS_COS)
    inv_t = lax.rsqrt(jnp.sum(target * target, axis=1, keepdims=True) + EPS_COS)
    cosine = jnp.sum(aligned * target, axis=1, keepdims=True) * inv_z * inv_t
    grad_aligned = -LAMBDA_ALIGN * (target * inv_t - cosine * aligned * inv_z) * inv_z
    grad_aligned = grad_aligned.astype(BF16)

    grad_second = (product_nt(grad_aligned, third_w) * second_slope).astype(BF16)
    third_term = product_tn(second_low, grad_aligned, BF16)
    third_sum = lax.psum_scatter(third_term, "seq", scatter_dimension=1, tiled=True)
    grad_seconds = gather_rows(grad_second)
    grad_firsts, sums = [], []
    for side in range(2):
        grad = product_nt(grad_seconds[side], second_w) * first_slopes[side]
        grad_firsts.append(grad.astype(BF16))
        sums.append(product_nt(grad_firsts[side], first_w, BF16))
    second_term = product_tn(
        jnp.concatenate(first_acts, 0), jnp.concatenate(grad_seconds, 0), BF16
    )
    second_third_sum = reduce_img(
        jnp.concatenate(
            [second_term.reshape(img, ph_cell, ph), third_sum.reshape(img, ph_cell, zd)], axis=2
        )
    )
    grad_first = jnp.concatenate(grad_firsts, 0)
    first_term = product_tn(jnp.concatenate(feed, 0), grad_first, BF16)
    grad_result = out_cotangent.astype(F32) + scatter_rows(*sums)

    grad_branch_b = (gate_b * grad_result).astype(BF16)
    grad_branches = gather_rows(grad_branch_b)
    grad_pres, sums = [], []
    for side in range(2):
        grad = product_nt(grad_branches[side], down_w) * slopes[side]
        grad_pres.append(grad.astype(BF16))
        sums.append(product_nt(grad_pres[side], up_w, BF16))
    down_term = product_tn(jnp.concatenate(acts, 0), jnp.concatenate(grad_branches, 0), BF16)
    down_first_sum = reduce_img(
        jnp.concatenate(
            [down_term.reshape(img, ff_cell, width), first_term.reshape(img, feat, ph_part)],
            axis=2,
        )
    )
    grad_pre = jnp.concatenate(grad_pres, 0)
    up_term = product_tn(jnp.concatenate(hidden_b, 0), grad_pre, BF16)
    grad_hidden_b = scatter_rows(*sums)
    grad_after = grad_result + norm_back(normed_b, inverse_b, grad_hidden_b * (1.0 + scale_b))

    grad_branch_a = (gate_a * grad_after).astype(BF16)
    grad_attended = product_nt(grad_branch_a, attn_w, BF16)
    attn_term = product_tn(attended, grad_branch_a, BF16)
    attn_sum = lax.psum_scatter(attn_term, "seq", scatter_dimension=1, tiled=True)
    attn_up_sum = reduce_img(
        jnp.concatenate(
            [attn_sum.reshape(img, feat, part_width), up_term.reshape(img, feat, ff_part)], axis=2
        )
    )
    grad_parts = grad_attended.reshape(own_rows, SEQ, part_width).transpose(1, 0, 2)
    grad_heads = [pick(grad_parts, place)]
    grad_heads += [swap(pick(grad_parts, place ^ p), p) for p in range(1, SEQ)]
    grad_heads = pad_heads(jnp.concatenate(grad_heads, 0))
    grad_q, grad_k, grad_v = attend_backward(qkv, grad_heads, block_slots)
    grad_qkv = jnp.concatenate([grad_q, grad_k, grad_v], axis=1)
    grad_hidden_a = scatter_rows(
        product_nt(grad_qkv[: 2 * own_rows], qkv_w, BF16),
        product_nt(grad_qkv[2 * own_rows :], qkv_w, BF16),
    )
    qkv_term = strip_heads(product_tn(hidden_a, grad_qkv, BF16))
    qkv_sum = reduce_img(qkv_term.reshape(img, feat, 3 * part_width))
    normed_a, inverse_a = norm_parts(tokens_f)
    tokens_grad = grad_after + norm_back(normed_a, inverse_a, grad_hidden_a * (1.0 + scale_a))

    own_sums = jnp.concatenate(
        [
            column_sums(grad_hidden_a),
            column_sums(grad_hidden_a * normed_a),
            column_sums(grad_after * branch_a),
            column_sums(grad_hidden_b),
            column_sums(grad_hidden_b * normed_b),
            column_sums(grad_result * branch_b),
        ]
    )
    by_place = [
        own_sums.reshape(SEQ, mod_cols),
        column_sums(grad_branch_a).reshape(SEQ, part_width),
        column_sums(grad_branch_b).reshape(SEQ, part_width),
        column_sums(grad_second).reshape(SEQ, ph_part),
        column_sums(grad_aligned).reshape(SEQ, zd // SEQ),
    ]
    seq_got = seq_exchange(jnp.concatenate(by_place, axis=1))
    all_slots = jnp.stack([slot_ids[p * own_rows] for p in range(SEQ)])
    member = (all_slots[None, :] == jnp.arange(slot_count, dtype=jnp.int32)[:, None]).astype(F32)
    grad_mod = jnp.sum(member[:, :, None] * seq_got[None, :, :mod_cols], axis=1)
    grad_mod = grad_mod.astype(BF16).astype(F32)
    row_biases = jnp.sum(seq_got[:, mod_cols:], axis=0)
    qkv_bias_sums = strip_heads(column_sums(grad_qkv))
    bias_sums = jnp.concatenate(
        [
            row_biases,
            qkv_bias_sums[:part_width],
            qkv_bias_sums[2 * part_width :],
            column_sums(grad_pre),
            column_sums(grad_first),
        ]
    )
    mod_size = slot_count * mod_cols
    img_got = img_gather(jnp.concatenate([grad_mod.reshape(mod_size), bias_sums]))
    grad_mods = img_got[:, :mod_size].reshape(img * slot_count, mod_cols).astype(BF16)
    bias_sums = jnp.sum(img_got[:, mod_size:], axis=0)
    ada_weight_grad = product_tn(cond_cols, grad_mods)
    cond_parts = product_nt(grad_mods, ada_weight).reshape(img, slot_count, feat)
    cond_parts = img_exchange(cond_parts).transpose(1, 0, 2).reshape(slot_count * width)
    last = jnp.concatenate([column_sums(grad_mods), bias_sums, cond_parts])
    last = lax.all_gather(last, "seq", axis=0, tiled=False)
    sizes = [mod_cols, part_width, part_width, ph_part, zd // SEQ, part_width, part_width]
    sizes += [ff_part, ph_part, slot_count * width]
    cuts, start = [], 0
    for size in sizes:
        cuts.append(last[:, start : start + size])
        start += size
    ada_bias_grad, attn_bias_grad, down_bias_grad, second_bias_grad, third_bias_grad = (
        cut.reshape(-1) for cut in cuts[:5]
    )
    query_bias_grad, value_bias_grad = cuts[5].reshape(-1), cuts[6].reshape(-1)
    up_bias_grad = cuts[7].reshape(SEQ, img, ff_cell).transpose(1, 0, 2).reshape(ff)
    first_bias_grad = cuts[8].reshape(SEQ, img, ph_cell).transpose(1, 0, 2).reshape(ph)
    conditioning_grad = jnp.sum(cuts[9], axis=0).reshape(slot_count, width) * cond_slope

    third_proj_grad = second_third_sum[:, ph:].reshape(ph // img, zd // SEQ)
    second_back = second_third_sum[:, :ph].astype(BF16).reshape(ph_cell, SEQ, ph_part)
    second_back = seq_exchange(second_back.transpose(1, 0, 2))
    second_proj_grad = second_back.reshape(ph // img, ph_part).astype(F32)

    down_back = down_first_sum[:, :width].reshape(ff_cell, SEQ, part_width).transpose(1, 0, 2)
    first_back = down_first_sum[:, width:].reshape(feat, SEQ, ph_part // SEQ).transpose(1, 0, 2)
    down_first_back = seq_exchange(jnp.concatenate([down_back, first_back], axis=2).astype(BF16))
    down_weight_grad = down_first_back[:, :, :part_width].reshape(ff // img, part_width)
    down_weight_grad = down_weight_grad.astype(F32)

    def cells_in_order(parts, cell):
        rows = parts.shape[1]
        parts = parts.reshape(SEQ, rows, img // SEQ, cell).transpose(1, 2, 0, 3)
        return parts.reshape(rows, img * cell).astype(F32)

    first_proj_grad = cells_in_order(down_first_back[:, :, part_width:], ph_cell)
    attn_weight_grad = attn_up_sum[:, :part_width]
    up_back = attn_up_sum[:, part_width:].astype(BF16).reshape(feat, SEQ, part_width)
    up_weight_grad = cells_in_order(seq_exchange(up_back.transpose(1, 0, 2)), ff_cell)

    kinds = qkv_sum.astype(BF16).reshape(feat, 3, part_width).transpose(1, 0, 2)
    qkv_back = seq_exchange(
        jnp.stack(
            [
                pick(kinds, jnp.minimum((3 * d + (place - 3 * d) % SEQ) // SEQ, 2))
                for d in range(SEQ)
            ]
        )
    )
    qkv_weight_grad = jnp.concatenate(
        [pick(qkv_back, (3 * place + j) % SEQ) for j in range(3)], axis=1
    ).astype(F32)

    return (
        feed_low,
        tokens_grad,
        conditioning_grad,
        ada_weight_grad,
        qkv_weight_grad,
        attn_weight_grad,
        up_weight_grad,
        down_weight_grad,
        first_proj_grad,
        second_proj_grad,
        third_proj_grad,
        ada_bias_grad,
        query_bias_grad,
        value_bias_grad,
        attn_bias_grad,
        up_bias_grad,
        down_bias_grad,
        first_bias_grad,
        second_bias_grad,
        third_bias_grad,
    )


def solution(mesh):
    rows = P(("img", "seq"), None)
    both = P("img", "seq")
    return jax.shard_map(
        local,
        mesh=mesh,
        in_specs=(rows, P("img", None), P("img"), rows, rows) + (both,) * 8 + (P(),) * 9,
        out_specs=(rows, rows, P("img", None)) + (both,) * 8 + (P(),) * 9,
        check_vma=False,
    )
```

```python
import jax
import jax.numpy as jnp
from jax import lax
from jax.experimental import pallas as pl
from jax.experimental.layout import Layout, with_layout_constraint
from jax.experimental.pallas import tpu as pltpu
from jax.sharding import PartitionSpec as P

H = 16
HD = 72
EPS_NORM = 1e-06
EPS_COS = 1e-06
LAMBDA_ALIGN = 0.5
MASKED_SCORE = -1e30
F32 = jnp.float32
BF16 = jnp.bfloat16
SEQ = 4


def product(left, right, out=F32):
    return lax.dot_general(
        left, right, (((1,), (0,)), ((), ())), preferred_element_type=F32
    ).astype(out)


def product_tn(left, right, out=F32):
    return lax.dot_general(
        left, right, (((0,), (0,)), ((), ())), preferred_element_type=F32
    ).astype(out)


def product_nt(left, right, out=F32):
    return lax.dot_general(
        left, right, (((1,), (1,)), ((), ())), preferred_element_type=F32
    ).astype(out)


def column_sums(values):
    return jnp.sum(values.astype(F32), axis=0)


def norm_parts(values):
    centered = values - jnp.mean(values, axis=-1, keepdims=True)
    inverse = lax.rsqrt(jnp.mean(centered * centered, axis=-1, keepdims=True) + EPS_NORM)
    return centered * inverse, inverse


def norm_back(normed, inverse, grad):
    return inverse * (
        grad
        - jnp.mean(grad, axis=-1, keepdims=True)
        - normed * jnp.mean(grad * normed, axis=-1, keepdims=True)
    )


def silu_parts(values):
    gate = 1.0 / (1.0 + jnp.exp(-values))
    return values * gate, gate * (1.0 + values * (1.0 - gate))


GELU_C = 0.7978845608028654


def gelu_parts(values):
    inner = GELU_C * (values + 0.044715 * values * values * values)
    bent = jnp.tanh(inner)
    slope = GELU_C * (1.0 + 3.0 * 0.044715 * values * values)
    value = 0.5 * values * (1.0 + bent)
    return value, 0.5 * (1.0 + bent) + 0.5 * values * (1.0 - bent * bent) * slope


def swap(values, distance):
    return lax.ppermute(values, "seq", [(i, i ^ distance) for i in range(SEQ)])


def gather_rows(own):
    across = swap(own, 2)
    near = swap(own, 1)
    far = swap(across, 1)
    return jnp.concatenate([own, near], 0), jnp.concatenate([across, far], 0)


def scatter_blocks(blocks):
    from_far = swap(blocks[3], 1)
    across = swap((blocks[2].astype(F32) + from_far.astype(F32)).astype(BF16), 2)
    from_near = swap(blocks[1], 1)
    return blocks[0].astype(F32) + from_near.astype(F32) + across.astype(F32)


def scatter_rows(near, far):
    rows = near.shape[0] // 2
    from_far = swap(far[rows:], 1)
    across = swap((far[:rows].astype(F32) + from_far.astype(F32)).astype(BF16), 2)
    from_near = swap(near[rows:], 1)
    return near[:rows].astype(F32) + from_near.astype(F32) + across.astype(F32)


def tie(value, *after):
    return lax.optimization_barrier((value,) + after)[0]


def img_swap(values):
    count = lax.axis_size("img")
    return lax.ppermute(values, "img", [(i, i ^ 1) for i in range(count)])


def slow_swap(values, distance):
    count = lax.axis_size("img")
    return lax.ppermute(values, "img", [(i, i ^ (2 * distance)) for i in range(count)])


def slow_groups():
    half = lax.axis_size("img") // 2
    return [[2 * k + fast for k in range(half)] for fast in range(2)]


def arrange(body, shapes, *arrays, place=None):
    outs = tuple(jax.ShapeDtypeStruct(shape, kind) for shape, kind in shapes)
    count = len(arrays)

    def kernel(where, *refs):
        body(where, refs[:count], refs[count:])

    whole = lambda array: pl.BlockSpec(array.shape, lambda step, where: (0,) * len(array.shape))
    where = jnp.zeros((1,), jnp.int32) if place is None else jnp.reshape(place, (-1,))
    return pl.pallas_call(
        kernel,
        grid_spec=pltpu.PrefetchScalarGridSpec(
            num_scalar_prefetch=1,
            grid=(1,),
            in_specs=[whole(array) for array in arrays],
            out_specs=tuple(whole(out) for out in outs),
        ),
        out_shape=outs,
        name="arrange",
    )(where.astype(jnp.int32), *arrays)


def join_columns(blocks, place=None):
    lead, cols = blocks[0].shape[:-1], blocks[0].shape[-1]

    def body(where, ins, outs):
        for turn in range(1 if place is None else SEQ):

            def put():
                for p, block in enumerate(ins):
                    at = (turn ^ p) * cols
                    outs[0][..., at : at + cols] = block[...]

            if place is None:
                put()
            else:
                pl.when(where[0] == turn)(put)

    return arrange(body, [(lead + (SEQ * cols,), blocks[0].dtype)], *blocks, place=place)[0]


def split_columns(values, place):
    rows, cols = values.shape[0], values.shape[1] // SEQ

    def body(where, ins, outs):
        for turn in range(SEQ):

            def put():
                for p in range(SEQ):
                    at = (turn ^ p) * cols
                    outs[p][...] = ins[0][:, at : at + cols]

            pl.when(where[0] == turn)(put)

    return arrange(body, [((rows, cols), values.dtype)] * SEQ, values, place=place)


def spread_img(shard):
    count = lax.axis_size("img")
    here = lax.axis_index("img")
    if count > 8:
        full = lax.all_gather(shard, "img", axis=0, tiled=False)
        return [full[k] for k in range(count)], jnp.arange(count, dtype=jnp.int32)
    blocks = []
    for k in range(count // 2):
        block = slow_swap(shard, k) if k else shard
        blocks += [block, img_swap(block)]
    return blocks, here ^ jnp.arange(count, dtype=jnp.int32)


def open_spread(body, shapes, blocks, where):
    def each(place, ins, outs):
        for k, block in enumerate(ins):
            body(block, *(out.at[place[k]] for out in outs))

    stacked = [((len(blocks),) + shape, BF16) for shape in shapes]
    return arrange(each, stacked, *blocks, place=where)


def open_blocks(body, shapes, stacked):
    count = stacked.shape[0]
    spec = lambda shape: pl.BlockSpec((1,) + shape, lambda i: (i,) + (0,) * len(shape))
    return pl.pallas_call(
        lambda ref, *outs: body(ref.at[0], *(out.at[0] for out in outs)),
        grid=(count,),
        in_specs=[spec(stacked.shape[1:])],
        out_specs=tuple(spec(shape) for shape in shapes),
        out_shape=tuple(jax.ShapeDtypeStruct((count,) + shape, BF16) for shape in shapes),
        name="open_blocks",
    )(stacked)


def reduce_pair(term, *after):
    count = lax.axis_size("img")
    rows = term.shape[0] // count
    fast = lax.axis_index("img") % 2
    pairs = term.reshape(count // 2, 2, rows, term.shape[1])
    send = lax.dynamic_index_in_dim(pairs, 1 - fast, 1, keepdims=False)
    keep = lax.dynamic_index_in_dim(pairs, fast, 1, keepdims=False)
    got = tie(img_swap(send), *after) if after else img_swap(send)
    return (keep.astype(F32) + got.astype(F32)).astype(BF16)


def slow_exchange(parts):
    return lax.all_to_all(
        parts, "img", split_axis=0, concat_axis=0, tiled=True, axis_index_groups=slow_groups()
    )


def block_sum(parts):
    return jnp.sum(parts.astype(F32), axis=0)


def slow_scatter(parts, *after):
    half = parts.shape[0]
    here = lax.axis_index("img") // 2
    if half > 4:
        return block_sum(slow_exchange(parts))
    got = [tie(slow_swap(pick(parts, here ^ k), k), *after) for k in range(1, half)]
    return sum((part.astype(F32) for part in got), pick(parts, here).astype(F32))


def seq_exchange(parts):
    return lax.all_to_all(parts, "seq", split_axis=0, concat_axis=0, tiled=True)


def img_exchange(parts):
    return lax.all_to_all(parts, "img", split_axis=0, concat_axis=0, tiled=True)


def img_gather(values):
    count = lax.axis_size("img")
    return img_exchange(jnp.broadcast_to(values[None], (count,) + values.shape))


def pick(stacked, index):
    return lax.dynamic_index_in_dim(stacked, index, 0, keepdims=False)


def block_probs(slots, block, queries, keys):
    rows = queries.shape[0]
    scores = lax.dot_general(queries, keys, (((1,), (1,)), ((), ())), preferred_element_type=F32)
    pieces = []
    for other in range(SEQ):
        piece = scores[:, other * rows : (other + 1) * rows] * HD ** (-0.5)
        pieces.append(jnp.where(slots[block] == slots[other], piece, MASKED_SCORE))
    scores = jnp.concatenate(pieces, axis=1)
    raised = jnp.exp(scores - jnp.max(scores, axis=1, keepdims=True))
    return raised * (1.0 / jnp.sum(raised, axis=1, keepdims=True))


def attend_kernel(slots, qkv_ref, out_ref):
    block = pl.program_id(0)
    rows, width = out_ref.shape
    first = pl.multiple_of(block * rows, rows)
    for start in range(0, width, HD):
        queries = qkv_ref[pl.ds(first, rows), start : start + HD]
        keys = qkv_ref[:, width + start : width + start + HD]
        values = qkv_ref[:, 2 * width + start : 2 * width + start + HD]
        probs = block_probs(slots, block, queries, keys)
        out_ref[:, start : start + HD] = jnp.dot(
            probs.astype(BF16), values, preferred_element_type=F32
        ).astype(BF16)


def attend_back_kernel(slots, qkv_ref, g_ref, out_ref, gk_sum, gv_sum):
    block = pl.program_id(0)
    rows, width = g_ref.shape
    scale = HD ** (-0.5)
    first = pl.multiple_of(block * rows, rows)

    @pl.when(block == 0)
    def _():
        gk_sum[...] = jnp.zeros_like(gk_sum)
        gv_sum[...] = jnp.zeros_like(gv_sum)

    for head in range(width // HD):
        start = head * HD
        queries = qkv_ref[pl.ds(first, rows), start : start + HD]
        keys = qkv_ref[:, width + start : width + start + HD]
        values = qkv_ref[:, 2 * width + start : 2 * width + start + HD]
        grads = g_ref[:, start : start + HD]
        probs = block_probs(slots, block, queries, keys)
        grad_probs = lax.dot_general(
            grads, values, (((1,), (1,)), ((), ())), preferred_element_type=F32
        )
        delta = jnp.sum(probs * grad_probs, axis=1, keepdims=True)
        grad_scores = (probs * (grad_probs - delta)).astype(BF16)
        out_ref[pl.ds(first, rows), start : start + HD] = (
            jnp.dot(grad_scores, keys, preferred_element_type=F32) * scale
        ).astype(BF16)
        gk_sum[head] += lax.dot_general(
            grad_scores, queries, (((0,), (0,)), ((), ())), preferred_element_type=F32
        )
        gv_sum[head] += lax.dot_general(
            probs.astype(BF16), grads, (((0,), (0,)), ((), ())), preferred_element_type=F32
        )

    @pl.when(block == SEQ - 1)
    def _():
        for head in range(width // HD):
            start = head * HD
            out_ref[:, width + start : width + start + HD] = (gk_sum[head] * scale).astype(BF16)
            out_ref[:, 2 * width + start : 2 * width + start + HD] = gv_sum[head].astype(BF16)


def attend_forward(qkv, slots):
    rows, width = qkv.shape[0], qkv.shape[1] // 3
    return pl.pallas_call(
        attend_kernel,
        grid_spec=pltpu.PrefetchScalarGridSpec(
            num_scalar_prefetch=1,
            grid=(SEQ,),
            in_specs=[pl.BlockSpec((rows, 3 * width), lambda block, slots: (0, 0))],
            out_specs=pl.BlockSpec((rows // SEQ, width), lambda block, slots: (block, 0)),
        ),
        out_shape=jax.ShapeDtypeStruct((rows, width), BF16),
        cost_estimate=pl.CostEstimate(
            flops=8 * rows * rows * width, bytes_accessed=8 * rows * width, transcendentals=rows * rows
        ),
        name="attend",
    )(slots, qkv)


def attend_backward(qkv, grads, slots):
    rows, width = grads.shape
    return pl.pallas_call(
        attend_back_kernel,
        grid_spec=pltpu.PrefetchScalarGridSpec(
            num_scalar_prefetch=1,
            grid=(SEQ,),
            in_specs=[
                pl.BlockSpec((rows, 3 * width), lambda block, slots: (0, 0)),
                pl.BlockSpec((rows // SEQ, width), lambda block, slots: (block, 0)),
            ],
            out_specs=pl.BlockSpec((rows, 3 * width), lambda block, slots: (0, 0)),
            scratch_shapes=[pltpu.VMEM((width // HD, rows, HD), F32)] * 2,
        ),
        out_shape=jax.ShapeDtypeStruct((rows, 3 * width), BF16),
        cost_estimate=pl.CostEstimate(
            flops=16 * rows * rows * width,
            bytes_accessed=16 * rows * width,
            transcendentals=rows * rows,
        ),
        name="attend_back",
    )(slots, qkv, grads)


def local(
    tokens,
    conditioning,
    slot_ids,
    dino_target,
    out_cotangent,
    ada_weight,
    qkv_weight,
    attn_weight,
    up_weight,
    down_weight,
    first_proj,
    second_proj,
    third_proj,
    ada_bias,
    query_bias,
    value_bias,
    attn_bias,
    up_bias,
    down_bias,
    first_bias,
    second_bias,
    third_bias,
):
    own_rows, width = tokens.shape
    place = lax.axis_index("seq")
    img = lax.axis_size("img")
    slot_count = conditioning.shape[0]
    part_width = width // SEQ
    feat = qkv_weight.shape[0]
    mod_cols = ada_weight.shape[1]
    ff = up_bias.shape[0]
    ph = first_bias.shape[0]
    zd = third_bias.shape[0]
    ff_part = ff // SEQ
    ph_part = ph // SEQ
    ff_cell = ff // img // SEQ
    ph_cell = ph // img // SEQ

    cond_act, cond_slope = silu_parts(conditioning)
    cond_low = cond_act.astype(BF16)
    cond_send = cond_low.reshape(slot_count, img, feat).transpose(1, 0, 2)
    cond_cols = img_exchange(cond_send).reshape(img * slot_count, feat)

    zd_part, third_rows = zd // SEQ, ph // img // 2

    zd_part, third_rows = zd // SEQ, ph // img // 2
    qkv_w = lax.all_gather(qkv_weight, "img", axis=0, tiled=True)
    swaps, swap_where = spread_img(attn_weight)

    rows_full = gather_rows(tokens)
    cells = img // SEQ
    first_width = ph_part // SEQ

    half = ph_part // 2
    first_at, second_at = 2 * part_width, 2 * part_width + first_width
    hidden_cols = second_at + half
    proj_cols = ph_part + SEQ * half

    def cut_hidden(where, ins, outs):
        up, down, first, second = ins
        for d in range(SEQ):
            for j in range(cells):
                at = (j * SEQ + d) * ff_cell
                outs[0][d, :, j * ff_cell : (j + 1) * ff_cell] = up[:, at : at + ff_cell]
                at, to = (j * SEQ + d) * ph_cell, first_at + j * ph_cell
                outs[0][d, :, to : to + ph_cell] = first[:, at : at + ph_cell]
            outs[0][d, :, part_width:first_at] = down[d]
            for side in range(2):
                rows = slice(side * ph_cell, (side + 1) * ph_cell)
                outs[0][d, rows, second_at:] = second[d, :, side * half : (side + 1) * half]

    mlp_send = arrange(
        cut_hidden,
        [((SEQ, feat, hidden_cols), BF16)],
        up_weight,
        down_weight.reshape(SEQ, ff_cell, part_width),
        first_proj,
        second_proj.reshape(SEQ, ph_cell, ph_part),
    )[0]

    def join_hidden(where, ins, outs):
        for d in range(SEQ):
            part = ins[0].at[d]
            at = d * part_width
            outs[0][:, at : at + part_width] = part[:, :part_width]
            at += ff_part
            outs[0][:, at : at + part_width] = part[:, part_width:first_at]
            at = d * first_width
            outs[1][:, at : at + first_width] = part[:, first_at:second_at]
            at = ph_part + d * half
            outs[1][:, at : at + half] = part[:, second_at:]
        for side in range(2):
            at = proj_cols + side * zd_part
            rows = slice(side * third_rows, (side + 1) * third_rows)
            outs[1][:third_rows, at : at + zd_part] = ins[1][rows]

    mod_send = product(cond_cols, ada_weight).reshape(img, slot_count, mod_cols)
    mod_parts = img_exchange(mod_send)
    my_bias = lax.dynamic_slice_in_dim(ada_bias, place * mod_cols, mod_cols, 0)
    mod_own = tie(jnp.sum(mod_parts, axis=0) + my_bias, *rows_full)
    modulation = lax.all_gather(mod_own, "seq", axis=1, tiled=True)
    mlp_got = seq_exchange(tie(mlp_send, modulation))
    mlp_shard, proj_shard = arrange(
        join_hidden,
        [((feat, 2 * ff_part), BF16), ((feat, proj_cols + 2 * zd_part), BF16)],
        mlp_got,
        third_proj,
    )
    mlp_all = lax.all_gather(mlp_shard, "img", axis=0, tiled=True)
    up_w, down_w = mlp_all[:, :ff_part], mlp_all[:, ff_part:]
    proj_all = lax.all_gather(proj_shard, "img", axis=0, tiled=True)
    proj_all = proj_all.reshape((img,) + proj_shard.shape)

    order = jnp.arange(SEQ, dtype=jnp.int32)
    all_slots = slot_ids.reshape(SEQ, own_rows)[:, 0]
    ours = (place ^ order)[:, None] == order[None, :]
    block_slots = jnp.sum(jnp.where(ours, all_slots[None, :], 0), axis=1)
    block_mod = sum(
        jnp.where((block_slots == slot)[:, None], modulation[slot][None, :], 0.0)
        for slot in range(slot_count)
    )
    shift_a, scale_a, gate_a, shift_b, scale_b, gate_b = jnp.split(block_mod[0], 6)

    def modulated(rows, first):
        normed, _ = norm_parts(rows.astype(F32).reshape(2, own_rows, width))
        shift = block_mod[first : first + 2, None, :width]
        scale = block_mod[first : first + 2, None, width : 2 * width]
        return (normed * (1.0 + scale) + shift).astype(BF16).reshape(2 * own_rows, width)

    hidden_a = jnp.concatenate([modulated(rows_full[0], 0), modulated(rows_full[1], 2)], 0)

    def open_attn(block, attn_ref):
        attn_ref[...] = block[...]

    def all_seq(part):
        across = swap(part, 2)
        return [part, swap(part, 1), across, swap(across, 1)]

    attn_part = open_spread(open_attn, [attn_weight.shape], swaps, swap_where)[0]
    attn_blocks = all_seq(attn_part)
    attn_w = join_columns(attn_blocks, place).reshape(width, width)
    zeros = jnp.zeros_like(query_bias)
    qkv_bias = jnp.concatenate([query_bias, zeros, value_bias])
    qkv_bias = lax.dynamic_slice_in_dim(qkv_bias, place * 3 * part_width, 3 * part_width, 0)
    qkv_own = (product(hidden_a, qkv_w) + qkv_bias).astype(BF16)

    distance = place ^ order
    chunk = (SEQ, own_rows, part_width)
    wide = (own_rows, SEQ * part_width)

    def cut_three(where, ins, outs):
        for turn in range(SEQ):

            def put():
                for p in range(SEQ):
                    rows = slice(p * own_rows, (p + 1) * own_rows)
                    at = (turn ^ p) * part_width
                    for j in range(3):
                        piece = ins[0][rows, j * part_width : (j + 1) * part_width]
                        outs[j][:, at : at + part_width] = piece

            pl.when(where[0] == turn)(put)

    turns = [[(i, (3 * i + j) % SEQ) for i in range(SEQ)] for j in range(3)]
    three = arrange(cut_three, [(wide, BF16)] * 3, qkv_own, place=place)
    three = [tie(lax.ppermute(three[j], "seq", turns[j]), *swaps) for j in range(3)]

    def join_three(where, ins, outs):
        for turn in range(3):

            def put():
                for kind in range(3):
                    at = kind * part_width
                    for b in range(SEQ):
                        piece = ins[(kind + turn) % 3][:, b * part_width : (b + 1) * part_width]
                        outs[0][b, :, at : at + part_width] = piece

            pl.when(where[0] == turn)(put)

    joined = (SEQ, own_rows, 3 * part_width)
    qkv = arrange(join_three, [(joined, BF16)], *three, place=place % 3)[0]
    qkv = qkv.reshape(SEQ * own_rows, 3 * part_width)
    attended_h = attend_forward(qkv, all_slots)

    def by_distance_rows(where, ins, outs):
        for p in range(SEQ):
            outs[p][...] = ins[0][where[p]]

    attended_h = arrange(
        by_distance_rows,
        [((own_rows, part_width), BF16)] * SEQ,
        attended_h.reshape(chunk),
        place=distance,
    )
    heads_rel = [attended_h[0]] + [swap(attended_h[p], p) for p in range(1, SEQ)]
    attended = join_columns([tie(block, attn_w) for block in heads_rel], place)
    tokens_f = tokens.astype(F32)
    branch_a = product(attended, attn_w) + attn_bias
    after_attn = tokens_f + gate_a * branch_a
    normed_b, inverse_b = norm_parts(after_attn)
    hidden_b = gather_rows((normed_b * (1.0 + scale_b) + shift_b).astype(BF16))

    my_up_bias = up_bias.reshape(img, SEQ, ff_cell)
    my_up_bias = lax.dynamic_index_in_dim(my_up_bias, place, 1, keepdims=False).reshape(ff_part)

    def open_projector(ref, first_ref, second_ref, third_ref):
        first_ref[...] = ref[:, :ph_part]
        for side in range(2):
            rows = slice(side * ph_cell, (side + 1) * ph_cell)
            for d in range(SEQ):
                at, to = ph_part + d * half, (2 * d + side) * half
                second_ref[:, to : to + half] = ref[rows, at : at + half]
            at = proj_cols + side * zd_part
            rows = slice(side * third_rows, (side + 1) * third_rows)
            third_ref[rows, :] = ref[:third_rows, at : at + zd_part]

    first_w, second_w, third_part = open_blocks(
        open_projector, [(feat, ph_part), (ph_cell, ph), (2 * third_rows, zd_part)], proj_all
    )
    first_w, second_w = first_w.reshape(width, ph_part), second_w.reshape(ph_part, ph)
    third_w = jnp.concatenate(all_seq(third_part.reshape(ph, zd_part).T), 0)
    acts, slopes, sums = [], [], []
    for side in range(2):
        value, slope = gelu_parts(product(hidden_b[side], up_w) + my_up_bias)
        acts.append(value.astype(BF16))
        slopes.append(slope)
        sums.append(product(acts[side], down_w, BF16))
    branch_b = scatter_rows(*sums) + down_bias
    result = after_attn + gate_b * branch_b
    feed_low = result.astype(BF16)

    feed = gather_rows(feed_low)
    my_first_bias = first_bias.reshape(img, SEQ, ph_cell)
    my_first_bias = lax.dynamic_index_in_dim(my_first_bias, place, 1, keepdims=False)
    my_first_bias = my_first_bias.reshape(ph_part)
    first_acts, first_slopes, sums = [], [], []
    for side in range(2):
        value, slope = silu_parts(product(feed[side], first_w) + my_first_bias)
        first_acts.append(value.astype(BF16))
        first_slopes.append(slope)
        sums.append(product(first_acts[side], second_w, BF16))
    second_act, second_slope = silu_parts(scatter_rows(*sums) + second_bias)
    second_low = second_act.astype(BF16)
    def by_distance(values):
        blocks = values.reshape(values.shape[:-1] + (SEQ, zd_part))
        blocks = [
            lax.dynamic_index_in_dim(blocks, place ^ p, blocks.ndim - 2, keepdims=False)
            for p in range(SEQ)
        ]
        return jnp.concatenate(blocks, axis=-1)

    aligned = product_nt(second_low, third_w) + by_distance(third_bias)
    target = join_columns(split_columns(dino_target, place)).astype(F32)
    inv_z = lax.rsqrt(jnp.sum(aligned * aligned, axis=1, keepdims=True) + EPS_COS)
    inv_t = lax.rsqrt(jnp.sum(target * target, axis=1, keepdims=True) + EPS_COS)
    cosine = jnp.sum(aligned * target, axis=1, keepdims=True) * inv_z * inv_t
    grad_aligned = -LAMBDA_ALIGN * (target * inv_t - cosine * aligned * inv_z) * inv_z
    grad_aligned = grad_aligned.astype(BF16)

    grad_second = (product(grad_aligned, third_w) * second_slope).astype(BF16)
    third_blocks = [
        product_tn(grad_aligned[:, p * zd_part : (p + 1) * zd_part], second_low, BF16)
        for p in range(SEQ)
    ]
    grad_seconds = gather_rows(grad_second)
    grad_firsts, sums = [], []
    for side in range(2):
        rows = grad_seconds[side] if side == 0 else tie(grad_seconds[1], sums[0], *third_blocks)
        grad = product_nt(rows, second_w) * first_slopes[side]
        grad_firsts.append(grad.astype(BF16))
        sums.append(product_nt(grad_firsts[side], first_w, BF16))
    first_acts = tie(jnp.concatenate(first_acts, 0), sums[1])
    second_term = product_tn(first_acts, jnp.concatenate(grad_seconds, 0), BF16)
    second_sum = lax.psum_scatter(second_term, "img", scatter_dimension=0, tiled=True)
    grad_first = jnp.concatenate(grad_firsts, 0)
    first_term = product_tn(tie(jnp.concatenate(feed, 0), sums[1]), grad_first, BF16)
    first_got = img_exchange(first_term.reshape(img, feat, ph_part))
    grad_result = tie(scatter_rows(*sums), second_term, first_term)
    grad_result = out_cotangent.astype(F32) + grad_result

    grad_branch_b = (gate_b * grad_result).astype(BF16)
    grad_branches = gather_rows(grad_branch_b)
    third_sum = scatter_blocks([tie(block, grad_branches[1]) for block in third_blocks])
    third_sum = third_sum.astype(BF16)
    grad_pres, sums = [], []
    for side in range(2):
        rows = grad_branches[side] if side == 0 else tie(grad_branches[1], sums[0], first_got)
        grad = product_nt(rows, down_w) * slopes[side]
        grad_pres.append(grad.astype(BF16))
        sums.append(product_nt(grad_pres[side], up_w, BF16))
    acts = tie(jnp.concatenate(acts, 0), sums[1])
    down_term = product_tn(acts, jnp.concatenate(grad_branches, 0), BF16)
    down_sum = lax.psum_scatter(down_term, "img", scatter_dimension=0, tiled=True)
    grad_pre = jnp.concatenate(grad_pres, 0)
    up_term = product_tn(tie(jnp.concatenate(hidden_b, 0), sums[1]), grad_pre, BF16)
    up_pair = reduce_pair(up_term)
    grad_hidden_b = tie(scatter_rows(*sums), down_term, up_term, third_sum)
    grad_after = grad_result + norm_back(normed_b, inverse_b, grad_hidden_b * (1.0 + scale_b))

    grad_branch_a = (gate_a * grad_after).astype(BF16)
    grad_attended = product_nt(tie(grad_branch_a, up_pair), attn_w, BF16)
    grad_parts = split_columns(grad_attended, place)
    grad_heads = [grad_parts[0]] + [swap(grad_parts[p], p) for p in range(1, SEQ)]
    branch_cols = split_columns(grad_branch_a, place)
    attended = tie(attended, *grad_parts)
    attn_sum = scatter_blocks([product_tn(attended, cols, BF16) for cols in branch_cols])
    up_got = slow_exchange(tie(up_pair, first_got))

    def rows_in_order(where, ins, outs):
        for p in range(SEQ):
            outs[0][where[p]] = ins[p][...]

    grad_heads = arrange(rows_in_order, [(chunk, BF16)], *grad_heads, place=distance)[0]
    grad_heads = grad_heads.reshape(SEQ * own_rows, part_width)
    grad_joined = attend_backward(qkv, grad_heads, all_slots)
    third_send = third_sum.reshape(zd_part, img, ph // img).transpose(1, 0, 2)
    third_got = img_exchange(tie(third_send, up_got))
    grad_joined = tie(grad_joined, up_got).reshape(joined)

    def cut_back(where, ins, outs):
        for turn in range(3):

            def put():
                for kind in range(3):
                    at = kind * part_width
                    for b in range(SEQ):
                        piece = ins[0][b, :, at : at + part_width]
                        outs[(kind + turn) % 3][:, b * part_width : (b + 1) * part_width] = piece

            pl.when(where[0] == turn)(put)

    backs = arrange(cut_back, [(wide, BF16)] * 3, grad_joined, place=place % 3)
    backs = [lax.ppermute(backs[j], "seq", [(b, a) for a, b in turns[j]]) for j in range(3)]
    backs = [tie(back, third_got) for back in backs]

    def join_back(where, ins, outs):
        for turn in range(SEQ):

            def put():
                for p in range(SEQ):
                    rows = slice(p * own_rows, (p + 1) * own_rows)
                    at = (turn ^ p) * part_width
                    for j in range(3):
                        piece = ins[j][:, at : at + part_width]
                        outs[0][rows, j * part_width : (j + 1) * part_width] = piece

            pl.when(where[0] == turn)(put)

    grad_qkv = arrange(join_back, [(qkv_own.shape, BF16)], *backs, place=place)[0]
    far = product_nt(grad_qkv[2 * own_rows :], qkv_w, BF16)
    near = product_nt(tie(grad_qkv, far)[: 2 * own_rows], qkv_w, BF16)
    grad_hidden_a = scatter_rows(near, far)
    qkv_term = product_tn(tie(hidden_a, near), grad_qkv, BF16)
    attn_send = attn_sum.astype(BF16).reshape(img, feat, part_width)
    attn_got = img_exchange(tie(attn_send, third_got))
    grad_hidden_a = tie(grad_hidden_a, attn_got)
    normed_a, inverse_a = norm_parts(tokens_f)
    tokens_grad = grad_after + norm_back(normed_a, inverse_a, grad_hidden_a * (1.0 + scale_a))

    own_sums = jnp.concatenate(
        [
            column_sums(grad_hidden_a),
            column_sums(grad_hidden_a * normed_a),
            column_sums(grad_after * branch_a),
            column_sums(grad_hidden_b),
            column_sums(grad_hidden_b * normed_b),
            column_sums(grad_result * branch_b),
        ]
    )
    aligned_sums = column_sums(grad_aligned).reshape(SEQ, zd_part)
    by_place = [
        own_sums.reshape(SEQ, mod_cols),
        column_sums(grad_branch_a).reshape(SEQ, part_width),
        column_sums(grad_branch_b).reshape(SEQ, part_width),
        column_sums(grad_second).reshape(SEQ, ph_part),
        jnp.stack([pick(aligned_sums, place ^ j) for j in range(SEQ)]),
    ]
    def split_sums(where, ins, outs):
        for d in range(SEQ):
            at = d * part_width
            total = ins[0][0, :, at : at + part_width].astype(F32)
            for k in range(1, img // 2):
                total = total + ins[0][k, :, at : at + part_width].astype(F32)
            outs[0][d, :, :part_width] = total.astype(BF16)
            outs[0][d, :, part_width:first_at] = ins[1][:, at : at + part_width]
            at = d * first_width
            total = ins[2][0, :, at : at + first_width].astype(F32)
            for k in range(1, img):
                total = total + ins[2][k, :, at : at + first_width].astype(F32)
            outs[0][d, :, first_at:second_at] = total.astype(BF16)
            for side in range(2):
                rows = slice(side * ph_cell, (side + 1) * ph_cell)
                at = (2 * d + side) * half
                outs[0][d, rows, second_at:] = ins[3][:, at : at + half]

    hidden_send = arrange(
        split_sums, [((SEQ, feat, hidden_cols), BF16)], up_got, down_sum, first_got, second_sum
    )[0]
    hidden_got = seq_exchange(tie(hidden_send, attn_got))

    by_place = jnp.concatenate(by_place, axis=1)
    seq_got = seq_exchange(tie(by_place, hidden_got))
    qkv_pair = reduce_pair(qkv_term, seq_got)
    member = (all_slots[None, :] == jnp.arange(slot_count, dtype=jnp.int32)[:, None]).astype(F32)
    grad_mod = jnp.sum(member[:, :, None] * seq_got[None, :, :mod_cols], axis=1)
    grad_mod = grad_mod.astype(BF16).astype(F32)
    row_biases = jnp.sum(seq_got[:, mod_cols:], axis=0)
    bias_sums = jnp.concatenate(
        [
            row_biases,
            column_sums(grad_qkv),
            column_sums(grad_pre),
            column_sums(grad_first),
        ]
    )
    mod_size = slot_count * mod_cols
    img_got = img_gather(jnp.concatenate([grad_mod.reshape(mod_size), bias_sums]))
    grad_mods = img_got[:, :mod_size].reshape(img * slot_count, mod_cols).astype(BF16)
    bias_sums = jnp.sum(img_got[:, mod_size:], axis=0)
    ada_weight_grad = product_tn(cond_cols, grad_mods)
    cond_parts = product_nt(grad_mods, ada_weight).reshape(img, slot_count, feat)
    qkv_weight_grad = slow_scatter(qkv_pair, img_got)
    cond_parts = img_exchange(cond_parts).transpose(1, 0, 2).reshape(slot_count * width)
    last = jnp.concatenate([column_sums(grad_mods), bias_sums, cond_parts])
    last = jnp.pad(last, (0, -last.shape[0] % 1024))
    last = lax.all_gather(last, "seq", axis=0, tiled=False)
    sizes = [mod_cols, part_width, part_width, ph_part, zd // SEQ, 3 * part_width]
    sizes += [ff_part, ph_part, slot_count * width]
    cuts, start = [], 0
    for size in sizes:
        cuts.append(last[:, start : start + size])
        start += size
    ada_bias_grad, attn_bias_grad, down_bias_grad, second_bias_grad, third_bias_grad = (
        cut.reshape(-1) for cut in cuts[:5]
    )
    qkv_bias_grad = cuts[5].reshape(-1)
    query_bias_grad, value_bias_grad = qkv_bias_grad[:width], qkv_bias_grad[2 * width :]
    up_bias_grad = cuts[6].reshape(SEQ, img, ff_cell).transpose(1, 0, 2).reshape(ff)
    first_bias_grad = cuts[7].reshape(SEQ, img, ph_cell).transpose(1, 0, 2).reshape(ph)
    conditioning_grad = jnp.sum(cuts[8], axis=0).reshape(slot_count, width) * cond_slope

    def join_cells(where, ins, outs):
        up, down, first, second = outs
        for d in range(SEQ):
            part = ins[0].at[d]
            for j in range(cells):
                at = (j * SEQ + d) * ff_cell
                up[:, at : at + ff_cell] = part[:, j * ff_cell : (j + 1) * ff_cell].astype(F32)
                at, to = (j * SEQ + d) * ph_cell, first_at + j * ph_cell
                first[:, at : at + ph_cell] = part[:, to : to + ph_cell].astype(F32)
            down[d] = part[:, part_width:first_at].astype(F32)
            for side in range(2):
                rows = slice(side * ph_cell, (side + 1) * ph_cell)
                second[d, :, side * half : (side + 1) * half] = part[rows, second_at:].astype(F32)

    up_weight_grad, down_weight_grad, first_proj_grad, second_proj_grad = arrange(
        join_cells,
        [
            ((feat, ff_part), F32),
            ((SEQ, ff_cell, part_width), F32),
            ((feat, ph_part), F32),
            ((SEQ, ph_cell, ph_part), F32),
        ],
        hidden_got,
    )
    down_weight_grad = down_weight_grad.reshape(ff // img, part_width)
    second_proj_grad = second_proj_grad.reshape(ph // img, ph_part)
    third_proj_grad = block_sum(third_got).T
    attn_weight_grad = block_sum(attn_got)
    return (
        feed_low,
        tokens_grad,
        conditioning_grad,
        ada_weight_grad,
        qkv_weight_grad,
        attn_weight_grad,
        up_weight_grad,
        down_weight_grad,
        first_proj_grad,
        second_proj_grad,
        third_proj_grad,
        ada_bias_grad,
        query_bias_grad,
        value_bias_grad,
        attn_bias_grad,
        up_bias_grad,
        down_bias_grad,
        first_bias_grad,
        second_bias_grad,
        third_bias_grad,
    )


def solution(mesh):
    rows = P(("img", "seq"), None)
    both = P("img", "seq")
    return jax.shard_map(
        local,
        mesh=mesh,
        in_specs=(rows, P("img", None), P("img"), rows, rows) + (both,) * 8 + (P(),) * 9,
        out_specs=(rows, rows, P("img", None)) + (both,) * 8 + (P(),) * 9,
        check_vma=False,
    )
```

```python
import jax
import jax.numpy as jnp
from jax import lax
from jax.experimental import pallas as pl
from jax.experimental.layout import Layout, with_layout_constraint
from jax.experimental.pallas import tpu as pltpu
from jax.sharding import PartitionSpec as P

H = 16
HD = 72
EPS_NORM = 1e-06
EPS_COS = 1e-06
LAMBDA_ALIGN = 0.5
MASKED_SCORE = -1e30
F32 = jnp.float32
BF16 = jnp.bfloat16
SEQ = 4


def product(left, right, out=F32):
    return lax.dot_general(
        left, right, (((1,), (0,)), ((), ())), preferred_element_type=F32
    ).astype(out)


def product_tn(left, right, out=F32):
    return lax.dot_general(
        left, right, (((0,), (0,)), ((), ())), preferred_element_type=F32
    ).astype(out)


def product_nt(left, right, out=F32):
    return lax.dot_general(
        left, right, (((1,), (1,)), ((), ())), preferred_element_type=F32
    ).astype(out)


def column_sums(values):
    return jnp.sum(values.astype(F32), axis=0)


def norm_parts(values):
    centered = values - jnp.mean(values, axis=-1, keepdims=True)
    inverse = lax.rsqrt(jnp.mean(centered * centered, axis=-1, keepdims=True) + EPS_NORM)
    return centered * inverse, inverse


def norm_back(normed, inverse, grad):
    return inverse * (
        grad
        - jnp.mean(grad, axis=-1, keepdims=True)
        - normed * jnp.mean(grad * normed, axis=-1, keepdims=True)
    )


def silu_parts(values):
    gate = 1.0 / (1.0 + jnp.exp(-values))
    return values * gate, gate * (1.0 + values * (1.0 - gate))


GELU_C = 0.7978845608028654


def gelu_parts(values):
    inner = GELU_C * (values + 0.044715 * values * values * values)
    bent = jnp.tanh(inner)
    slope = GELU_C * (1.0 + 3.0 * 0.044715 * values * values)
    value = 0.5 * values * (1.0 + bent)
    return value, 0.5 * (1.0 + bent) + 0.5 * values * (1.0 - bent * bent) * slope


def swap(values, distance):
    return lax.ppermute(values, "seq", [(i, i ^ distance) for i in range(SEQ)])


def gather_rows(own):
    across = swap(own, 2)
    near = swap(own, 1)
    far = swap(across, 1)
    return jnp.concatenate([own, near], 0), jnp.concatenate([across, far], 0)


def scatter_blocks(blocks, *after):
    from_far = swap(blocks[3], 1)
    pair = (blocks[2].astype(F32) + from_far.astype(F32)).astype(BF16)
    across = swap(tie(pair, *after) if after else pair, 2)
    from_near = swap(blocks[1], 1)
    return blocks[0].astype(F32) + from_near.astype(F32) + across.astype(F32)


def scatter_rows(near, far):
    rows = near.shape[0] // 2
    from_far = swap(far[rows:], 1)
    across = swap((far[:rows].astype(F32) + from_far.astype(F32)).astype(BF16), 2)
    from_near = swap(near[rows:], 1)
    return near[:rows].astype(F32) + from_near.astype(F32) + across.astype(F32)


def tie(value, *after):
    return lax.optimization_barrier((value,) + after)[0]


def img_swap(values):
    count = lax.axis_size("img")
    return lax.ppermute(values, "img", [(i, i ^ 1) for i in range(count)])


def slow_swap(values, distance):
    count = lax.axis_size("img")
    return lax.ppermute(values, "img", [(i, i ^ (2 * distance)) for i in range(count)])


def slow_groups():
    half = lax.axis_size("img") // 2
    return [[2 * k + fast for k in range(half)] for fast in range(2)]


def arrange(body, shapes, *arrays, place=None):
    outs = tuple(jax.ShapeDtypeStruct(shape, kind) for shape, kind in shapes)
    count = len(arrays)

    def kernel(where, *refs):
        body(where, refs[:count], refs[count:])

    whole = lambda array: pl.BlockSpec(array.shape, lambda step, where: (0,) * len(array.shape))
    where = jnp.zeros((1,), jnp.int32) if place is None else jnp.reshape(place, (-1,))
    return pl.pallas_call(
        kernel,
        grid_spec=pltpu.PrefetchScalarGridSpec(
            num_scalar_prefetch=1,
            grid=(1,),
            in_specs=[whole(array) for array in arrays],
            out_specs=tuple(whole(out) for out in outs),
        ),
        out_shape=outs,
        name="arrange",
    )(where.astype(jnp.int32), *arrays)


def join_columns(blocks, place=None):
    lead, cols = blocks[0].shape[:-1], blocks[0].shape[-1]

    def body(where, ins, outs):
        for turn in range(1 if place is None else SEQ):

            def put():
                for p, block in enumerate(ins):
                    at = (turn ^ p) * cols
                    outs[0][..., at : at + cols] = block[...]

            if place is None:
                put()
            else:
                pl.when(where[0] == turn)(put)

    return arrange(body, [(lead + (SEQ * cols,), blocks[0].dtype)], *blocks, place=place)[0]


def split_columns(values, place):
    rows, cols = values.shape[0], values.shape[1] // SEQ

    def body(where, ins, outs):
        for turn in range(SEQ):

            def put():
                for p in range(SEQ):
                    at = (turn ^ p) * cols
                    outs[p][...] = ins[0][:, at : at + cols]

            pl.when(where[0] == turn)(put)

    return arrange(body, [((rows, cols), values.dtype)] * SEQ, values, place=place)


def spread_img(shard):
    count = lax.axis_size("img")
    here = lax.axis_index("img")
    if count > 8:
        full = lax.all_gather(shard, "img", axis=0, tiled=False)
        return [full[k] for k in range(count)], jnp.arange(count, dtype=jnp.int32)
    blocks = []
    for k in range(count // 2):
        block = slow_swap(shard, k) if k else shard
        blocks += [block, img_swap(block)]
    return blocks, here ^ jnp.arange(count, dtype=jnp.int32)


def open_spread(body, shapes, blocks, where):
    def each(place, ins, outs):
        for k, block in enumerate(ins):
            body(block, *(out.at[place[k]] for out in outs))

    stacked = [((len(blocks),) + shape, BF16) for shape in shapes]
    return arrange(each, stacked, *blocks, place=where)


def open_blocks(body, shapes, stacked):
    count = stacked.shape[0]
    spec = lambda shape: pl.BlockSpec((1,) + shape, lambda i: (i,) + (0,) * len(shape))
    return pl.pallas_call(
        lambda ref, *outs: body(ref.at[0], *(out.at[0] for out in outs)),
        grid=(count,),
        in_specs=[spec(stacked.shape[1:])],
        out_specs=tuple(spec(shape) for shape in shapes),
        out_shape=tuple(jax.ShapeDtypeStruct((count,) + shape, BF16) for shape in shapes),
        name="open_blocks",
    )(stacked)


def pair_send(blocks):
    count, rows, cols = blocks.shape
    fast = lax.axis_index("img") % 2
    pairs = blocks.reshape(count // 2, 2, rows, cols)
    return img_swap(lax.dynamic_index_in_dim(pairs, 1 - fast, 1, keepdims=False))


def pair_sum(terms, gots):
    count, rows = terms[0].shape[:2]
    cols = [term.shape[2] for term in terms]

    def body(where, ins, outs):
        for k in range(count // 2):
            at = 0
            for j, size in enumerate(cols):
                kept = ins[j][2 * k + where[0]].astype(F32)
                total = kept + ins[len(cols) + j][k].astype(F32)
                outs[0][k, :, at : at + size] = total.astype(BF16)
                at += size

    fast = lax.axis_index("img") % 2
    shape = (count // 2, rows, sum(cols))
    return arrange(body, [(shape, BF16)], *terms, *gots, place=fast)[0]


def slow_exchange(parts):
    return lax.all_to_all(
        parts, "img", split_axis=0, concat_axis=0, tiled=True, axis_index_groups=slow_groups()
    )


def block_sum(parts):
    return jnp.sum(parts.astype(F32), axis=0)


def slow_scatter(parts, *after):
    half = parts.shape[0]
    here = lax.axis_index("img") // 2
    if half > 4:
        return block_sum(slow_exchange(parts))
    got = [tie(slow_swap(pick(parts, here ^ k), k), *after) for k in range(1, half)]
    return sum((part.astype(F32) for part in got), pick(parts, here).astype(F32))


def seq_exchange(parts):
    return lax.all_to_all(parts, "seq", split_axis=0, concat_axis=0, tiled=True)


def img_exchange(parts):
    return lax.all_to_all(parts, "img", split_axis=0, concat_axis=0, tiled=True)


def img_gather(values):
    count = lax.axis_size("img")
    return img_exchange(jnp.broadcast_to(values[None], (count,) + values.shape))


def pick(stacked, index):
    return lax.dynamic_index_in_dim(stacked, index, 0, keepdims=False)


def block_probs(slots, block, queries, keys):
    rows = queries.shape[0]
    scores = lax.dot_general(queries, keys, (((1,), (1,)), ((), ())), preferred_element_type=F32)
    pieces = []
    for other in range(SEQ):
        piece = scores[:, other * rows : (other + 1) * rows] * HD ** (-0.5)
        pieces.append(jnp.where(slots[block] == slots[other], piece, MASKED_SCORE))
    scores = jnp.concatenate(pieces, axis=1)
    raised = jnp.exp(scores - jnp.max(scores, axis=1, keepdims=True))
    return raised * (1.0 / jnp.sum(raised, axis=1, keepdims=True))


def attend_kernel(slots, qkv_ref, out_ref):
    block = pl.program_id(0)
    rows, width = out_ref.shape
    first = pl.multiple_of(block * rows, rows)
    for start in range(0, width, HD):
        queries = qkv_ref[pl.ds(first, rows), start : start + HD]
        keys = qkv_ref[:, width + start : width + start + HD]
        values = qkv_ref[:, 2 * width + start : 2 * width + start + HD]
        probs = block_probs(slots, block, queries, keys)
        out_ref[:, start : start + HD] = jnp.dot(
            probs.astype(BF16), values, preferred_element_type=F32
        ).astype(BF16)


def attend_back_kernel(slots, qkv_ref, g_ref, out_ref, gk_sum, gv_sum):
    block = pl.program_id(0)
    rows, width = g_ref.shape
    scale = HD ** (-0.5)
    first = pl.multiple_of(block * rows, rows)

    @pl.when(block == 0)
    def _():
        gk_sum[...] = jnp.zeros_like(gk_sum)
        gv_sum[...] = jnp.zeros_like(gv_sum)

    for head in range(width // HD):
        start = head * HD
        queries = qkv_ref[pl.ds(first, rows), start : start + HD]
        keys = qkv_ref[:, width + start : width + start + HD]
        values = qkv_ref[:, 2 * width + start : 2 * width + start + HD]
        grads = g_ref[:, start : start + HD]
        probs = block_probs(slots, block, queries, keys)
        grad_probs = lax.dot_general(
            grads, values, (((1,), (1,)), ((), ())), preferred_element_type=F32
        )
        delta = jnp.sum(probs * grad_probs, axis=1, keepdims=True)
        grad_scores = (probs * (grad_probs - delta)).astype(BF16)
        out_ref[pl.ds(first, rows), start : start + HD] = (
            jnp.dot(grad_scores, keys, preferred_element_type=F32) * scale
        ).astype(BF16)
        gk_sum[head] += lax.dot_general(
            grad_scores, queries, (((0,), (0,)), ((), ())), preferred_element_type=F32
        )
        gv_sum[head] += lax.dot_general(
            probs.astype(BF16), grads, (((0,), (0,)), ((), ())), preferred_element_type=F32
        )

    @pl.when(block == SEQ - 1)
    def _():
        for head in range(width // HD):
            start = head * HD
            out_ref[:, width + start : width + start + HD] = (gk_sum[head] * scale).astype(BF16)
            out_ref[:, 2 * width + start : 2 * width + start + HD] = gv_sum[head].astype(BF16)


def attend_forward(qkv, slots):
    rows, width = qkv.shape[0], qkv.shape[1] // 3
    return pl.pallas_call(
        attend_kernel,
        grid_spec=pltpu.PrefetchScalarGridSpec(
            num_scalar_prefetch=1,
            grid=(SEQ,),
            in_specs=[pl.BlockSpec((rows, 3 * width), lambda block, slots: (0, 0))],
            out_specs=pl.BlockSpec((rows // SEQ, width), lambda block, slots: (block, 0)),
        ),
        out_shape=jax.ShapeDtypeStruct((rows, width), BF16),
        cost_estimate=pl.CostEstimate(
            flops=8 * rows * rows * width, bytes_accessed=8 * rows * width, transcendentals=rows * rows
        ),
        name="attend",
    )(slots, qkv)


def attend_backward(qkv, grads, slots):
    rows, width = grads.shape
    return pl.pallas_call(
        attend_back_kernel,
        grid_spec=pltpu.PrefetchScalarGridSpec(
            num_scalar_prefetch=1,
            grid=(SEQ,),
            in_specs=[
                pl.BlockSpec((rows, 3 * width), lambda block, slots: (0, 0)),
                pl.BlockSpec((rows // SEQ, width), lambda block, slots: (block, 0)),
            ],
            out_specs=pl.BlockSpec((rows, 3 * width), lambda block, slots: (0, 0)),
            scratch_shapes=[pltpu.VMEM((width // HD, rows, HD), F32)] * 2,
        ),
        out_shape=jax.ShapeDtypeStruct((rows, 3 * width), BF16),
        cost_estimate=pl.CostEstimate(
            flops=16 * rows * rows * width,
            bytes_accessed=16 * rows * width,
            transcendentals=rows * rows,
        ),
        name="attend_back",
    )(slots, qkv, grads)


def local(
    tokens,
    conditioning,
    slot_ids,
    dino_target,
    out_cotangent,
    ada_weight,
    qkv_weight,
    attn_weight,
    up_weight,
    down_weight,
    first_proj,
    second_proj,
    third_proj,
    ada_bias,
    query_bias,
    value_bias,
    attn_bias,
    up_bias,
    down_bias,
    first_bias,
    second_bias,
    third_bias,
):
    own_rows, width = tokens.shape
    place = lax.axis_index("seq")
    img = lax.axis_size("img")
    slot_count = conditioning.shape[0]
    part_width = width // SEQ
    feat = qkv_weight.shape[0]
    mod_cols = ada_weight.shape[1]
    ff = up_bias.shape[0]
    ph = first_bias.shape[0]
    zd = third_bias.shape[0]
    ff_part = ff // SEQ
    ph_part = ph // SEQ
    ff_cell = ff // img // SEQ
    ph_cell = ph // img // SEQ

    cond_act, cond_slope = silu_parts(conditioning)
    cond_low = cond_act.astype(BF16)
    cond_send = cond_low.reshape(slot_count, img, feat).transpose(1, 0, 2)
    cond_cols = img_exchange(cond_send).reshape(img * slot_count, feat)

    zd_part, third_rows = zd // SEQ, ph // img // 2

    zd_part, third_rows = zd // SEQ, ph // img // 2
    qkv_w = lax.all_gather(qkv_weight, "img", axis=0, tiled=True)
    swaps, swap_where = spread_img(attn_weight)

    rows_full = gather_rows(tokens)
    cells = img // SEQ
    first_width = ph_part // SEQ

    half = ph_part // 2
    first_at, second_at = 2 * part_width, 2 * part_width + first_width
    hidden_cols = second_at + half
    proj_cols = ph_part + SEQ * half

    def cut_hidden(where, ins, outs):
        up, down, first, second = ins
        for d in range(SEQ):
            for j in range(cells):
                at = (j * SEQ + d) * ff_cell
                outs[0][d, :, j * ff_cell : (j + 1) * ff_cell] = up[:, at : at + ff_cell]
                at, to = (j * SEQ + d) * ph_cell, first_at + j * ph_cell
                outs[0][d, :, to : to + ph_cell] = first[:, at : at + ph_cell]
            outs[0][d, :, part_width:first_at] = down[d]
            for side in range(2):
                rows = slice(side * ph_cell, (side + 1) * ph_cell)
                outs[0][d, rows, second_at:] = second[d, :, side * half : (side + 1) * half]

    mlp_send = arrange(
        cut_hidden,
        [((SEQ, feat, hidden_cols), BF16)],
        up_weight,
        down_weight.reshape(SEQ, ff_cell, part_width),
        first_proj,
        second_proj.reshape(SEQ, ph_cell, ph_part),
    )[0]

    def join_hidden(where, ins, outs):
        for d in range(SEQ):
            part = ins[0].at[d]
            at = d * part_width
            outs[0][:, at : at + part_width] = part[:, :part_width]
            at += ff_part
            outs[0][:, at : at + part_width] = part[:, part_width:first_at]
            at = d * first_width
            outs[1][:, at : at + first_width] = part[:, first_at:second_at]
            at = ph_part + d * half
            outs[1][:, at : at + half] = part[:, second_at:]
        for side in range(2):
            at = proj_cols + side * zd_part
            rows = slice(side * third_rows, (side + 1) * third_rows)
            outs[1][:third_rows, at : at + zd_part] = ins[1][rows]

    mod_send = product(cond_cols, ada_weight).reshape(img, slot_count, mod_cols)
    mod_parts = img_exchange(mod_send)
    my_bias = lax.dynamic_slice_in_dim(ada_bias, place * mod_cols, mod_cols, 0)
    mod_own = tie(jnp.sum(mod_parts, axis=0) + my_bias, *rows_full)
    modulation = lax.all_gather(mod_own, "seq", axis=1, tiled=True)
    mlp_got = seq_exchange(tie(mlp_send, modulation))
    mlp_shard, proj_shard = arrange(
        join_hidden,
        [((feat, 2 * ff_part), BF16), ((feat, proj_cols + 2 * zd_part), BF16)],
        mlp_got,
        third_proj,
    )
    mlp_all = lax.all_gather(mlp_shard, "img", axis=0, tiled=True)
    up_w, down_w = mlp_all[:, :ff_part], mlp_all[:, ff_part:]
    proj_all = lax.all_gather(proj_shard, "img", axis=0, tiled=True)
    proj_all = proj_all.reshape((img,) + proj_shard.shape)

    order = jnp.arange(SEQ, dtype=jnp.int32)
    all_slots = slot_ids.reshape(SEQ, own_rows)[:, 0]
    ours = (place ^ order)[:, None] == order[None, :]
    block_slots = jnp.sum(jnp.where(ours, all_slots[None, :], 0), axis=1)
    block_mod = sum(
        jnp.where((block_slots == slot)[:, None], modulation[slot][None, :], 0.0)
        for slot in range(slot_count)
    )
    shift_a, scale_a, gate_a, shift_b, scale_b, gate_b = jnp.split(block_mod[0], 6)

    def modulated(rows, first):
        normed, _ = norm_parts(rows.astype(F32).reshape(2, own_rows, width))
        shift = block_mod[first : first + 2, None, :width]
        scale = block_mod[first : first + 2, None, width : 2 * width]
        return (normed * (1.0 + scale) + shift).astype(BF16).reshape(2 * own_rows, width)

    hidden_a = jnp.concatenate([modulated(rows_full[0], 0), modulated(rows_full[1], 2)], 0)

    def open_attn(block, attn_ref):
        attn_ref[...] = block[...]

    def all_seq(part):
        across = swap(part, 2)
        return [part, swap(part, 1), across, swap(across, 1)]

    attn_part = open_spread(open_attn, [attn_weight.shape], swaps, swap_where)[0]
    attn_blocks = all_seq(attn_part)
    attn_w = join_columns(attn_blocks, place).reshape(width, width)
    zeros = jnp.zeros_like(query_bias)
    qkv_bias = jnp.concatenate([query_bias, zeros, value_bias])
    qkv_bias = lax.dynamic_slice_in_dim(qkv_bias, place * 3 * part_width, 3 * part_width, 0)
    qkv_own = (product(hidden_a, qkv_w) + qkv_bias).astype(BF16)

    distance = place ^ order
    chunk = (SEQ, own_rows, part_width)
    wide = (own_rows, SEQ * part_width)

    def cut_three(where, ins, outs):
        for turn in range(SEQ):

            def put():
                for p in range(SEQ):
                    rows = slice(p * own_rows, (p + 1) * own_rows)
                    at = (turn ^ p) * part_width
                    for j in range(3):
                        piece = ins[0][rows, j * part_width : (j + 1) * part_width]
                        outs[j][:, at : at + part_width] = piece

            pl.when(where[0] == turn)(put)

    turns = [[(i, (3 * i + j) % SEQ) for i in range(SEQ)] for j in range(3)]
    three = arrange(cut_three, [(wide, BF16)] * 3, qkv_own, place=place)
    three = [tie(lax.ppermute(three[j], "seq", turns[j]), *swaps) for j in range(3)]

    def join_three(where, ins, outs):
        for turn in range(3):

            def put():
                for kind in range(3):
                    at = kind * part_width
                    for b in range(SEQ):
                        piece = ins[(kind + turn) % 3][:, b * part_width : (b + 1) * part_width]
                        outs[0][b, :, at : at + part_width] = piece

            pl.when(where[0] == turn)(put)

    joined = (SEQ, own_rows, 3 * part_width)
    qkv = arrange(join_three, [(joined, BF16)], *three, place=place % 3)[0]
    qkv = qkv.reshape(SEQ * own_rows, 3 * part_width)
    attended_h = attend_forward(qkv, all_slots)

    def by_distance_rows(where, ins, outs):
        for p in range(SEQ):
            outs[p][...] = ins[0][where[p]]

    attended_h = arrange(
        by_distance_rows,
        [((own_rows, part_width), BF16)] * SEQ,
        attended_h.reshape(chunk),
        place=distance,
    )
    heads_rel = [attended_h[0]] + [swap(attended_h[p], p) for p in range(1, SEQ)]
    attended = join_columns([tie(block, attn_w) for block in heads_rel], place)
    tokens_f = tokens.astype(F32)
    branch_a = product(attended, attn_w) + attn_bias
    after_attn = tokens_f + gate_a * branch_a
    normed_b, inverse_b = norm_parts(after_attn)
    hidden_b = gather_rows((normed_b * (1.0 + scale_b) + shift_b).astype(BF16))

    my_up_bias = up_bias.reshape(img, SEQ, ff_cell)
    my_up_bias = lax.dynamic_index_in_dim(my_up_bias, place, 1, keepdims=False).reshape(ff_part)

    def open_projector(ref, first_ref, second_ref, third_ref):
        first_ref[...] = ref[:, :ph_part]
        for side in range(2):
            rows = slice(side * ph_cell, (side + 1) * ph_cell)
            for d in range(SEQ):
                at, to = ph_part + d * half, (2 * d + side) * half
                second_ref[:, to : to + half] = ref[rows, at : at + half]
            at = proj_cols + side * zd_part
            rows = slice(side * third_rows, (side + 1) * third_rows)
            third_ref[rows, :] = ref[:third_rows, at : at + zd_part]

    first_w, second_w, third_part = open_blocks(
        open_projector, [(feat, ph_part), (ph_cell, ph), (2 * third_rows, zd_part)], proj_all
    )
    first_w, second_w = first_w.reshape(width, ph_part), second_w.reshape(ph_part, ph)
    third_w = jnp.concatenate(all_seq(third_part.reshape(ph, zd_part).T), 0)
    acts, slopes, sums = [], [], []
    for side in range(2):
        value, slope = gelu_parts(product(hidden_b[side], up_w) + my_up_bias)
        acts.append(value.astype(BF16))
        slopes.append(slope)
        sums.append(product(acts[side], down_w, BF16))
    branch_b = scatter_rows(*sums) + down_bias
    result = after_attn + gate_b * branch_b
    feed_low = result.astype(BF16)

    feed = gather_rows(feed_low)
    my_first_bias = first_bias.reshape(img, SEQ, ph_cell)
    my_first_bias = lax.dynamic_index_in_dim(my_first_bias, place, 1, keepdims=False)
    my_first_bias = my_first_bias.reshape(ph_part)
    first_acts, first_slopes, sums = [], [], []
    for side in range(2):
        value, slope = silu_parts(product(feed[side], first_w) + my_first_bias)
        first_acts.append(value.astype(BF16))
        first_slopes.append(slope)
        sums.append(product(first_acts[side], second_w, BF16))
    second_act, second_slope = silu_parts(scatter_rows(*sums) + second_bias)
    second_low = second_act.astype(BF16)
    def by_distance(values):
        blocks = values.reshape(values.shape[:-1] + (SEQ, zd_part))
        blocks = [
            lax.dynamic_index_in_dim(blocks, place ^ p, blocks.ndim - 2, keepdims=False)
            for p in range(SEQ)
        ]
        return jnp.concatenate(blocks, axis=-1)

    aligned = product_nt(second_low, third_w) + by_distance(third_bias)
    target = join_columns(split_columns(dino_target, place)).astype(F32)
    inv_z = lax.rsqrt(jnp.sum(aligned * aligned, axis=1, keepdims=True) + EPS_COS)
    inv_t = lax.rsqrt(jnp.sum(target * target, axis=1, keepdims=True) + EPS_COS)
    cosine = jnp.sum(aligned * target, axis=1, keepdims=True) * inv_z * inv_t
    grad_aligned = -LAMBDA_ALIGN * (target * inv_t - cosine * aligned * inv_z) * inv_z
    grad_aligned = grad_aligned.astype(BF16)

    grad_second = (product(grad_aligned, third_w) * second_slope).astype(BF16)
    third_blocks = [
        product_tn(second_low, grad_aligned[:, p * zd_part : (p + 1) * zd_part], BF16)
        for p in range(SEQ)
    ]
    grad_seconds = gather_rows(grad_second)
    third_sum = scatter_blocks(third_blocks, grad_seconds[1]).astype(BF16)
    grad_firsts, sums = [], []
    for side in range(2):
        rows = grad_seconds[side] if side == 0 else tie(grad_seconds[1], sums[0], *third_blocks)
        grad = product_nt(rows, second_w) * first_slopes[side]
        grad_firsts.append(grad.astype(BF16))
        sums.append(product_nt(grad_firsts[side], first_w, BF16))
    first_acts = tie(jnp.concatenate(first_acts, 0), sums[1], third_sum)
    second_term = product_tn(first_acts, jnp.concatenate(grad_seconds, 0), BF16)
    second_sum = lax.psum_scatter(second_term, "img", scatter_dimension=0, tiled=True)
    grad_first = jnp.concatenate(grad_firsts, 0)
    first_term = product_tn(tie(jnp.concatenate(feed, 0), sums[1]), grad_first, BF16)
    first_got = img_exchange(first_term.reshape(img, feat, ph_part))
    grad_result = tie(scatter_rows(*sums), second_term, first_term)
    grad_result = out_cotangent.astype(F32) + grad_result

    grad_branch_b = (gate_b * grad_result).astype(BF16)
    grad_branches = gather_rows(grad_branch_b)

    def pack_third(where, ins, outs):
        for i in range(img):
            for side in range(2):
                first = (2 * i + side) * third_rows
                at = side * zd_part
                outs[0][i, :third_rows, at : at + zd_part] = ins[0][first : first + third_rows]

    third_shape = (img, feat, 2 * zd_part)
    third_blocks = arrange(pack_third, [(third_shape, BF16)], third_sum)[0]
    third_half = pair_send(third_blocks)
    grad_pres, sums = [], []
    for side in range(2):
        rows = grad_branches[side] if side == 0 else tie(grad_branches[1], sums[0], first_got)
        grad = product_nt(rows, down_w) * slopes[side]
        grad_pres.append(grad.astype(BF16))
        sums.append(product_nt(grad_pres[side], up_w, BF16))
    acts = tie(jnp.concatenate(acts, 0), sums[1])
    down_term = product_tn(acts, jnp.concatenate(grad_branches, 0), BF16)
    down_sum = lax.psum_scatter(down_term, "img", scatter_dimension=0, tiled=True)
    grad_pre = jnp.concatenate(grad_pres, 0)
    up_term = product_tn(tie(jnp.concatenate(hidden_b, 0), sums[1]), grad_pre, BF16)
    up_blocks = up_term.reshape(img, feat, ff_part)
    up_half = pair_send(up_blocks)
    grad_hidden_b = tie(scatter_rows(*sums), down_term, up_term)
    grad_after = grad_result + norm_back(normed_b, inverse_b, grad_hidden_b * (1.0 + scale_b))

    grad_branch_a = (gate_a * grad_after).astype(BF16)
    grad_attended = product_nt(grad_branch_a, attn_w, BF16)
    grad_parts = split_columns(grad_attended, place)
    grad_heads = [grad_parts[0]] + [swap(grad_parts[p], p) for p in range(1, SEQ)]
    branch_cols = split_columns(grad_branch_a, place)
    attended = tie(attended, *grad_parts)
    attn_sum = scatter_blocks(
        [product_tn(attended, cols, BF16) for cols in branch_cols]
    ).astype(BF16)
    attn_sum = attn_sum.reshape(img, feat, part_width)
    attn_half = pair_send(attn_sum)
    up_pair = pair_sum([up_blocks, third_blocks], [tie(up_half, *grad_parts), third_half])
    up_got = slow_exchange(tie(up_pair, first_got))

    def rows_in_order(where, ins, outs):
        for p in range(SEQ):
            outs[0][where[p]] = ins[p][...]

    grad_heads = arrange(rows_in_order, [(chunk, BF16)], *grad_heads, place=distance)[0]
    grad_heads = grad_heads.reshape(SEQ * own_rows, part_width)
    grad_joined = attend_backward(qkv, grad_heads, all_slots)
    grad_joined = tie(grad_joined, attn_sum).reshape(joined)

    def cut_back(where, ins, outs):
        for turn in range(3):

            def put():
                for kind in range(3):
                    at = kind * part_width
                    for b in range(SEQ):
                        piece = ins[0][b, :, at : at + part_width]
                        outs[(kind + turn) % 3][:, b * part_width : (b + 1) * part_width] = piece

            pl.when(where[0] == turn)(put)

    backs = arrange(cut_back, [(wide, BF16)] * 3, grad_joined, place=place % 3)
    backs = [lax.ppermute(backs[j], "seq", [(b, a) for a, b in turns[j]]) for j in range(3)]
    backs = [tie(back, up_got) for back in backs]

    def join_back(where, ins, outs):
        for turn in range(SEQ):

            def put():
                for p in range(SEQ):
                    rows = slice(p * own_rows, (p + 1) * own_rows)
                    at = (turn ^ p) * part_width
                    for j in range(3):
                        piece = ins[j][:, at : at + part_width]
                        outs[0][rows, j * part_width : (j + 1) * part_width] = piece

            pl.when(where[0] == turn)(put)

    grad_qkv = arrange(join_back, [(qkv_own.shape, BF16)], *backs, place=place)[0]
    far = product_nt(grad_qkv[2 * own_rows :], qkv_w, BF16)
    qkv_term = product_tn(tie(hidden_a, far), grad_qkv, BF16)
    near = product_nt(tie(grad_qkv, qkv_term)[: 2 * own_rows], qkv_w, BF16)
    grad_hidden_a = scatter_rows(near, far)
    qkv_blocks = qkv_term.reshape(img, feat, 3 * part_width)
    normed_a, inverse_a = norm_parts(tokens_f)
    tokens_grad = grad_after + norm_back(normed_a, inverse_a, grad_hidden_a * (1.0 + scale_a))

    own_sums = jnp.concatenate(
        [
            column_sums(grad_hidden_a),
            column_sums(grad_hidden_a * normed_a),
            column_sums(grad_after * branch_a),
            column_sums(grad_hidden_b),
            column_sums(grad_hidden_b * normed_b),
            column_sums(grad_result * branch_b),
        ]
    )
    aligned_sums = column_sums(grad_aligned).reshape(SEQ, zd_part)
    by_place = [
        own_sums.reshape(SEQ, mod_cols),
        column_sums(grad_branch_a).reshape(SEQ, part_width),
        column_sums(grad_branch_b).reshape(SEQ, part_width),
        column_sums(grad_second).reshape(SEQ, ph_part),
        jnp.stack([pick(aligned_sums, place ^ j) for j in range(SEQ)]),
    ]
    by_place = jnp.concatenate(by_place, axis=1)
    seq_got = seq_exchange(by_place)
    qkv_half = tie(pair_send(qkv_blocks), seq_got)
    qkv_pair = pair_sum([qkv_blocks, attn_sum], [qkv_half, attn_half])
    member = (all_slots[None, :] == jnp.arange(slot_count, dtype=jnp.int32)[:, None]).astype(F32)
    grad_mod = jnp.sum(member[:, :, None] * seq_got[None, :, :mod_cols], axis=1)
    row_biases = jnp.sum(seq_got[:, mod_cols:], axis=0)
    bias_sums = jnp.concatenate(
        [
            row_biases,
            column_sums(grad_qkv),
            column_sums(grad_pre),
            column_sums(grad_first),
        ]
    )
    mod_size = slot_count * mod_cols
    leading = lax.reduce_precision(bias_sums, 8, 7)
    rest = bias_sums - leading
    packed = [grad_mod.reshape(mod_size), leading, rest]
    img_got = img_gather(jnp.concatenate([part.astype(BF16) for part in packed]))
    grad_mods = img_got[:, :mod_size].reshape(img * slot_count, mod_cols)
    bias_pairs = img_got[:, mod_size:].astype(F32).reshape(img * 2, bias_sums.shape[0])
    bias_sums = jnp.sum(bias_pairs, axis=0)
    ada_weight_grad = product_tn(cond_cols, grad_mods)
    cond_parts = product_nt(grad_mods, ada_weight).reshape(img, slot_count, feat)
    cond_parts = img_exchange(cond_parts).transpose(1, 0, 2).reshape(slot_count * width)
    def split_sums(where, ins, outs):
        for d in range(SEQ):
            at = d * part_width
            total = ins[0][0, :, at : at + part_width].astype(F32)
            for k in range(1, img // 2):
                total = total + ins[0][k, :, at : at + part_width].astype(F32)
            outs[0][d, :, :part_width] = total.astype(BF16)
            outs[0][d, :, part_width:first_at] = ins[1][:, at : at + part_width]
            at = d * first_width
            total = ins[2][0, :, at : at + first_width].astype(F32)
            for k in range(1, img):
                total = total + ins[2][k, :, at : at + first_width].astype(F32)
            outs[0][d, :, first_at:second_at] = total.astype(BF16)
            for side in range(2):
                rows = slice(side * ph_cell, (side + 1) * ph_cell)
                at = (2 * d + side) * half
                outs[0][d, rows, second_at:] = ins[3][:, at : at + half]

    hidden_send = arrange(
        split_sums, [((SEQ, feat, hidden_cols), BF16)], tie(up_got, near), down_sum, first_got, second_sum
    )[0]
    hidden_got = [swap(pick(hidden_send, place ^ p), p) for p in range(1, SEQ)]
    hidden_got = [pick(hidden_send, place)] + hidden_got

    def in_order(where, ins, outs):
        for p in range(SEQ):
            outs[0][where[p]] = ins[p][...]

    hidden_got = [tie(block, img_got) for block in hidden_got]
    hidden_got = arrange(in_order, [(hidden_send.shape, BF16)], *hidden_got, place=distance)[0]

    qkv_attn_grad = slow_scatter(qkv_pair, cond_parts)
    qkv_weight_grad = qkv_attn_grad[:, : 3 * part_width]
    attn_weight_grad = qkv_attn_grad[:, 3 * part_width :]
    last = jnp.concatenate([column_sums(grad_mods), bias_sums, cond_parts])
    last = jnp.pad(last, (0, -last.shape[0] % 1024))
    last = lax.all_gather(last, "seq", axis=0, tiled=False)
    sizes = [mod_cols, part_width, part_width, ph_part, zd // SEQ, 3 * part_width]
    sizes += [ff_part, ph_part, slot_count * width]
    cuts, start = [], 0
    for size in sizes:
        cuts.append(last[:, start : start + size])
        start += size
    ada_bias_grad, attn_bias_grad, down_bias_grad, second_bias_grad, third_bias_grad = (
        cut.reshape(-1) for cut in cuts[:5]
    )
    qkv_bias_grad = cuts[5].reshape(-1)
    query_bias_grad, value_bias_grad = qkv_bias_grad[:width], qkv_bias_grad[2 * width :]
    up_bias_grad = cuts[6].reshape(SEQ, img, ff_cell).transpose(1, 0, 2).reshape(ff)
    first_bias_grad = cuts[7].reshape(SEQ, img, ph_cell).transpose(1, 0, 2).reshape(ph)
    conditioning_grad = jnp.sum(cuts[8], axis=0).reshape(slot_count, width) * cond_slope

    def join_cells(where, ins, outs):
        up, down, first, second = outs
        for d in range(SEQ):
            part = ins[0].at[d]
            for j in range(cells):
                at = (j * SEQ + d) * ff_cell
                up[:, at : at + ff_cell] = part[:, j * ff_cell : (j + 1) * ff_cell].astype(F32)
                at, to = (j * SEQ + d) * ph_cell, first_at + j * ph_cell
                first[:, at : at + ph_cell] = part[:, to : to + ph_cell].astype(F32)
            down[d] = part[:, part_width:first_at].astype(F32)
            for side in range(2):
                rows = slice(side * ph_cell, (side + 1) * ph_cell)
                second[d, :, side * half : (side + 1) * half] = part[rows, second_at:].astype(F32)

    up_weight_grad, down_weight_grad, first_proj_grad, second_proj_grad = arrange(
        join_cells,
        [
            ((feat, ff_part), F32),
            ((SEQ, ff_cell, part_width), F32),
            ((feat, ph_part), F32),
            ((SEQ, ph_cell, ph_part), F32),
        ],
        hidden_got,
    )
    down_weight_grad = down_weight_grad.reshape(ff // img, part_width)
    second_proj_grad = second_proj_grad.reshape(ph // img, ph_part)

    def open_third(where, ins, outs):
        for side in range(2):
            at = ff_part + side * zd_part
            total = ins[0][0, :third_rows, at : at + zd_part].astype(F32)
            for k in range(1, img // 2):
                total = total + ins[0][k, :third_rows, at : at + zd_part].astype(F32)
            outs[0][side * third_rows : (side + 1) * third_rows] = total

    third_proj_grad = arrange(open_third, [(third_proj.shape, F32)], tie(up_got, img_got))[0]
    return (
        feed_low,
        tokens_grad,
        conditioning_grad,
        ada_weight_grad,
        qkv_weight_grad,
        attn_weight_grad,
        up_weight_grad,
        down_weight_grad,
        first_proj_grad,
        second_proj_grad,
        third_proj_grad,
        ada_bias_grad,
        query_bias_grad,
        value_bias_grad,
        attn_bias_grad,
        up_bias_grad,
        down_bias_grad,
        first_bias_grad,
        second_bias_grad,
        third_bias_grad,
    )


def solution(mesh):
    rows = P(("img", "seq"), None)
    both = P("img", "seq")
    return jax.shard_map(
        local,
        mesh=mesh,
        in_specs=(rows, P("img", None), P("img"), rows, rows) + (both,) * 8 + (P(),) * 9,
        out_specs=(rows, rows, P("img", None)) + (both,) * 8 + (P(),) * 9,
        check_vma=False,
    )
```

```python
import jax
import jax.numpy as jnp
from jax import lax
from jax.experimental import pallas as pl
from jax.experimental.layout import Layout, with_layout_constraint
from jax.experimental.pallas import tpu as pltpu
from jax.sharding import PartitionSpec as P

H = 16
HD = 72
EPS_NORM = 1e-06
EPS_COS = 1e-06
LAMBDA_ALIGN = 0.5
MASKED_SCORE = -1e30
F32 = jnp.float32
BF16 = jnp.bfloat16
SEQ = 4


def product(left, right, out=F32):
    return lax.dot_general(
        left, right, (((1,), (0,)), ((), ())), preferred_element_type=F32
    ).astype(out)


def product_tn(left, right, out=F32):
    return lax.dot_general(
        left, right, (((0,), (0,)), ((), ())), preferred_element_type=F32
    ).astype(out)


def product_nt(left, right, out=F32):
    return lax.dot_general(
        left, right, (((1,), (1,)), ((), ())), preferred_element_type=F32
    ).astype(out)


def column_sums(values):
    return jnp.sum(values.astype(F32), axis=0)


def norm_parts(values):
    centered = values - jnp.mean(values, axis=-1, keepdims=True)
    inverse = lax.rsqrt(jnp.mean(centered * centered, axis=-1, keepdims=True) + EPS_NORM)
    return centered * inverse, inverse


def norm_back(normed, inverse, grad):
    return inverse * (
        grad
        - jnp.mean(grad, axis=-1, keepdims=True)
        - normed * jnp.mean(grad * normed, axis=-1, keepdims=True)
    )


def silu_parts(values):
    gate = 1.0 / (1.0 + jnp.exp(-values))
    return values * gate, gate * (1.0 + values * (1.0 - gate))


GELU_C = 0.7978845608028654


def gelu_parts(values):
    inner = GELU_C * (values + 0.044715 * values * values * values)
    bent = jnp.tanh(inner)
    slope = GELU_C * (1.0 + 3.0 * 0.044715 * values * values)
    value = 0.5 * values * (1.0 + bent)
    return value, 0.5 * (1.0 + bent) + 0.5 * values * (1.0 - bent * bent) * slope


def swap(values, distance):
    return lax.ppermute(values, "seq", [(i, i ^ distance) for i in range(SEQ)])


def gather_rows(own):
    across = swap(own, 2)
    near = swap(own, 1)
    far = swap(across, 1)
    return jnp.concatenate([own, near], 0), jnp.concatenate([across, far], 0)


def scatter_blocks(blocks, *after):
    from_far = swap(blocks[3], 1)
    pair = (blocks[2].astype(F32) + from_far.astype(F32)).astype(BF16)
    across = swap(tie(pair, *after) if after else pair, 2)
    from_near = swap(blocks[1], 1)
    return blocks[0].astype(F32) + from_near.astype(F32) + across.astype(F32)


def scatter_rows(near, far):
    rows = near.shape[0] // 2
    from_far = swap(far[rows:], 1)
    across = swap((far[:rows].astype(F32) + from_far.astype(F32)).astype(BF16), 2)
    from_near = swap(near[rows:], 1)
    return near[:rows].astype(F32) + from_near.astype(F32) + across.astype(F32)


def tie(value, *after):
    return lax.optimization_barrier((value,) + after)[0]


def img_swap(values):
    count = lax.axis_size("img")
    return lax.ppermute(values, "img", [(i, i ^ 1) for i in range(count)])


def slow_swap(values, distance):
    count = lax.axis_size("img")
    return lax.ppermute(values, "img", [(i, i ^ (2 * distance)) for i in range(count)])


def slow_groups():
    half = lax.axis_size("img") // 2
    return [[2 * k + fast for k in range(half)] for fast in range(2)]


def arrange(body, shapes, *arrays, place=None):
    outs = tuple(jax.ShapeDtypeStruct(shape, kind) for shape, kind in shapes)
    count = len(arrays)

    def kernel(where, *refs):
        body(where, refs[:count], refs[count:])

    whole = lambda array: pl.BlockSpec(array.shape, lambda step, where: (0,) * len(array.shape))
    where = jnp.zeros((1,), jnp.int32) if place is None else jnp.reshape(place, (-1,))
    return pl.pallas_call(
        kernel,
        grid_spec=pltpu.PrefetchScalarGridSpec(
            num_scalar_prefetch=1,
            grid=(1,),
            in_specs=[whole(array) for array in arrays],
            out_specs=tuple(whole(out) for out in outs),
        ),
        out_shape=outs,
        name="arrange",
    )(where.astype(jnp.int32), *arrays)


def join_columns(blocks, place=None):
    lead, cols = blocks[0].shape[:-1], blocks[0].shape[-1]

    def body(where, ins, outs):
        for turn in range(1 if place is None else SEQ):

            def put():
                for p, block in enumerate(ins):
                    at = (turn ^ p) * cols
                    outs[0][..., at : at + cols] = block[...]

            if place is None:
                put()
            else:
                pl.when(where[0] == turn)(put)

    return arrange(body, [(lead + (SEQ * cols,), blocks[0].dtype)], *blocks, place=place)[0]


def split_columns(values, place):
    rows, cols = values.shape[0], values.shape[1] // SEQ

    def body(where, ins, outs):
        for turn in range(SEQ):

            def put():
                for p in range(SEQ):
                    at = (turn ^ p) * cols
                    outs[p][...] = ins[0][:, at : at + cols]

            pl.when(where[0] == turn)(put)

    return arrange(body, [((rows, cols), values.dtype)] * SEQ, values, place=place)


def spread_img(shard):
    count = lax.axis_size("img")
    here = lax.axis_index("img")
    if count > 8:
        full = lax.all_gather(shard, "img", axis=0, tiled=False)
        return [full[k] for k in range(count)], jnp.arange(count, dtype=jnp.int32)
    blocks = []
    for k in range(count // 2):
        block = slow_swap(shard, k) if k else shard
        blocks += [block, img_swap(block)]
    return blocks, here ^ jnp.arange(count, dtype=jnp.int32)


def open_spread(body, shapes, blocks, where):
    def each(place, ins, outs):
        for k, block in enumerate(ins):
            body(block, *(out.at[place[k]] for out in outs))

    stacked = [((len(blocks),) + shape, BF16) for shape in shapes]
    return arrange(each, stacked, *blocks, place=where)


def open_blocks(body, shapes, stacked):
    count = stacked.shape[0]
    spec = lambda shape: pl.BlockSpec((1,) + shape, lambda i: (i,) + (0,) * len(shape))
    return pl.pallas_call(
        lambda ref, *outs: body(ref.at[0], *(out.at[0] for out in outs)),
        grid=(count,),
        in_specs=[spec(stacked.shape[1:])],
        out_specs=tuple(spec(shape) for shape in shapes),
        out_shape=tuple(jax.ShapeDtypeStruct((count,) + shape, BF16) for shape in shapes),
        name="open_blocks",
    )(stacked)


def pair_send(blocks):
    count, rows, cols = blocks.shape
    fast = lax.axis_index("img") % 2
    pairs = blocks.reshape(count // 2, 2, rows, cols)
    return img_swap(lax.dynamic_index_in_dim(pairs, 1 - fast, 1, keepdims=False))


def pair_sum(terms, gots):
    count, rows = terms[0].shape[:2]
    cols = [term.shape[2] for term in terms]

    def body(where, ins, outs):
        for k in range(count // 2):
            at = 0
            for j, size in enumerate(cols):
                kept = ins[j][2 * k + where[0]].astype(F32)
                total = kept + ins[len(cols) + j][k].astype(F32)
                outs[0][k, :, at : at + size] = total.astype(BF16)
                at += size

    fast = lax.axis_index("img") % 2
    shape = (count // 2, rows, sum(cols))
    return arrange(body, [(shape, BF16)], *terms, *gots, place=fast)[0]


def slow_exchange(parts):
    return lax.all_to_all(
        parts, "img", split_axis=0, concat_axis=0, tiled=True, axis_index_groups=slow_groups()
    )


def block_sum(parts):
    return jnp.sum(parts.astype(F32), axis=0)


def slow_scatter(parts, *after):
    half = parts.shape[0]
    here = lax.axis_index("img") // 2
    if half > 4:
        return block_sum(slow_exchange(parts))
    got = [tie(slow_swap(pick(parts, here ^ k), k), *after) for k in range(1, half)]
    return sum((part.astype(F32) for part in got), pick(parts, here).astype(F32))


def seq_exchange(parts):
    return lax.all_to_all(parts, "seq", split_axis=0, concat_axis=0, tiled=True)


def img_exchange(parts):
    return lax.all_to_all(parts, "img", split_axis=0, concat_axis=0, tiled=True)


def img_gather(values):
    count = lax.axis_size("img")
    return img_exchange(jnp.broadcast_to(values[None], (count,) + values.shape))


def pick(stacked, index):
    return lax.dynamic_index_in_dim(stacked, index, 0, keepdims=False)


def block_probs(slots, block, queries, keys):
    rows = queries.shape[0]
    scores = lax.dot_general(queries, keys, (((1,), (1,)), ((), ())), preferred_element_type=F32)
    pieces = []
    for other in range(SEQ):
        piece = scores[:, other * rows : (other + 1) * rows] * HD ** (-0.5)
        pieces.append(jnp.where(slots[block] == slots[other], piece, MASKED_SCORE))
    scores = jnp.concatenate(pieces, axis=1)
    raised = jnp.exp(scores - jnp.max(scores, axis=1, keepdims=True))
    return raised * (1.0 / jnp.sum(raised, axis=1, keepdims=True))


def attend_kernel(slots, qkv_ref, out_ref):
    block = pl.program_id(0)
    rows, width = out_ref.shape
    first = pl.multiple_of(block * rows, rows)
    for start in range(0, width, HD):
        queries = qkv_ref[pl.ds(first, rows), start : start + HD]
        keys = qkv_ref[:, width + start : width + start + HD]
        values = qkv_ref[:, 2 * width + start : 2 * width + start + HD]
        probs = block_probs(slots, block, queries, keys)
        out_ref[:, start : start + HD] = jnp.dot(
            probs.astype(BF16), values, preferred_element_type=F32
        ).astype(BF16)


def attend_back_kernel(slots, qkv_ref, g_ref, out_ref, gk_sum, gv_sum):
    block = pl.program_id(0)
    rows, width = g_ref.shape
    scale = HD ** (-0.5)
    first = pl.multiple_of(block * rows, rows)

    @pl.when(block == 0)
    def _():
        gk_sum[...] = jnp.zeros_like(gk_sum)
        gv_sum[...] = jnp.zeros_like(gv_sum)

    for head in range(width // HD):
        start = head * HD
        queries = qkv_ref[pl.ds(first, rows), start : start + HD]
        keys = qkv_ref[:, width + start : width + start + HD]
        values = qkv_ref[:, 2 * width + start : 2 * width + start + HD]
        grads = g_ref[:, start : start + HD]
        probs = block_probs(slots, block, queries, keys)
        grad_probs = lax.dot_general(
            grads, values, (((1,), (1,)), ((), ())), preferred_element_type=F32
        )
        delta = jnp.sum(probs * grad_probs, axis=1, keepdims=True)
        grad_scores = (probs * (grad_probs - delta)).astype(BF16)
        out_ref[pl.ds(first, rows), start : start + HD] = (
            jnp.dot(grad_scores, keys, preferred_element_type=F32) * scale
        ).astype(BF16)
        gk_sum[head] += lax.dot_general(
            grad_scores, queries, (((0,), (0,)), ((), ())), preferred_element_type=F32
        )
        gv_sum[head] += lax.dot_general(
            probs.astype(BF16), grads, (((0,), (0,)), ((), ())), preferred_element_type=F32
        )

    @pl.when(block == SEQ - 1)
    def _():
        for head in range(width // HD):
            start = head * HD
            out_ref[:, width + start : width + start + HD] = (gk_sum[head] * scale).astype(BF16)
            out_ref[:, 2 * width + start : 2 * width + start + HD] = gv_sum[head].astype(BF16)


def attend_forward(qkv, slots):
    rows, width = qkv.shape[0], qkv.shape[1] // 3
    return pl.pallas_call(
        attend_kernel,
        grid_spec=pltpu.PrefetchScalarGridSpec(
            num_scalar_prefetch=1,
            grid=(SEQ,),
            in_specs=[pl.BlockSpec((rows, 3 * width), lambda block, slots: (0, 0))],
            out_specs=pl.BlockSpec((rows // SEQ, width), lambda block, slots: (block, 0)),
        ),
        out_shape=jax.ShapeDtypeStruct((rows, width), BF16),
        cost_estimate=pl.CostEstimate(
            flops=8 * rows * rows * width, bytes_accessed=8 * rows * width, transcendentals=rows * rows
        ),
        name="attend",
    )(slots, qkv)


def attend_backward(qkv, grads, slots):
    rows, width = grads.shape
    return pl.pallas_call(
        attend_back_kernel,
        grid_spec=pltpu.PrefetchScalarGridSpec(
            num_scalar_prefetch=1,
            grid=(SEQ,),
            in_specs=[
                pl.BlockSpec((rows, 3 * width), lambda block, slots: (0, 0)),
                pl.BlockSpec((rows // SEQ, width), lambda block, slots: (block, 0)),
            ],
            out_specs=pl.BlockSpec((rows, 3 * width), lambda block, slots: (0, 0)),
            scratch_shapes=[pltpu.VMEM((width // HD, rows, HD), F32)] * 2,
        ),
        out_shape=jax.ShapeDtypeStruct((rows, 3 * width), BF16),
        cost_estimate=pl.CostEstimate(
            flops=16 * rows * rows * width,
            bytes_accessed=16 * rows * width,
            transcendentals=rows * rows,
        ),
        name="attend_back",
    )(slots, qkv, grads)


def local(
    tokens,
    conditioning,
    slot_ids,
    dino_target,
    out_cotangent,
    ada_weight,
    qkv_weight,
    attn_weight,
    up_weight,
    down_weight,
    first_proj,
    second_proj,
    third_proj,
    ada_bias,
    query_bias,
    value_bias,
    attn_bias,
    up_bias,
    down_bias,
    first_bias,
    second_bias,
    third_bias,
):
    own_rows, width = tokens.shape
    place = lax.axis_index("seq")
    img = lax.axis_size("img")
    slot_count = conditioning.shape[0]
    part_width = width // SEQ
    feat = qkv_weight.shape[0]
    mod_cols = ada_weight.shape[1]
    ff = up_bias.shape[0]
    ph = first_bias.shape[0]
    zd = third_bias.shape[0]
    ff_part = ff // SEQ
    ph_part = ph // SEQ
    ff_cell = ff // img // SEQ
    ph_cell = ph // img // SEQ

    cond_act, cond_slope = silu_parts(conditioning)
    cond_low = cond_act.astype(BF16)
    cond_send = cond_low.reshape(slot_count, img, feat).transpose(1, 0, 2)
    cond_cols = img_exchange(cond_send).reshape(img * slot_count, feat)

    zd_part, third_rows = zd // SEQ, ph // img // 2

    zd_part, third_rows = zd // SEQ, ph // img // 2
    qkv_w = lax.all_gather(qkv_weight, "img", axis=0, tiled=True)
    swaps, swap_where = spread_img(attn_weight)

    rows_full = gather_rows(tokens)
    cells = img // SEQ
    first_width = ph_part // SEQ

    half = ph_part // 2
    first_at, second_at = 2 * part_width, 2 * part_width + first_width
    hidden_cols = second_at + half
    proj_cols = ph_part + SEQ * half

    def cut_hidden(where, ins, outs):
        up, down, first, second = ins
        for d in range(SEQ):
            for j in range(cells):
                at = (j * SEQ + d) * ff_cell
                outs[0][d, :, j * ff_cell : (j + 1) * ff_cell] = up[:, at : at + ff_cell]
                at, to = (j * SEQ + d) * ph_cell, first_at + j * ph_cell
                outs[0][d, :, to : to + ph_cell] = first[:, at : at + ph_cell]
            outs[0][d, :, part_width:first_at] = down[d]
            for side in range(2):
                rows = slice(side * ph_cell, (side + 1) * ph_cell)
                outs[0][d, rows, second_at:] = second[d, :, side * half : (side + 1) * half]

    mlp_send = arrange(
        cut_hidden,
        [((SEQ, feat, hidden_cols), BF16)],
        up_weight,
        down_weight.reshape(SEQ, ff_cell, part_width),
        first_proj,
        second_proj.reshape(SEQ, ph_cell, ph_part),
    )[0]

    def join_hidden(where, ins, outs):
        for d in range(SEQ):
            part = ins[0].at[d]
            at = d * part_width
            outs[0][:, at : at + part_width] = part[:, :part_width]
            at += ff_part
            outs[0][:, at : at + part_width] = part[:, part_width:first_at]
            at = d * first_width
            outs[1][:, at : at + first_width] = part[:, first_at:second_at]
            at = ph_part + d * half
            outs[1][:, at : at + half] = part[:, second_at:]
        for side in range(2):
            at = proj_cols + side * zd_part
            rows = slice(side * third_rows, (side + 1) * third_rows)
            outs[1][:third_rows, at : at + zd_part] = ins[1][rows]

    mod_send = product(cond_cols, ada_weight).reshape(img, slot_count, mod_cols)
    mod_parts = img_exchange(mod_send)
    my_bias = lax.dynamic_slice_in_dim(ada_bias, place * mod_cols, mod_cols, 0)
    mod_own = tie(jnp.sum(mod_parts, axis=0) + my_bias, *rows_full)
    modulation = lax.all_gather(mod_own, "seq", axis=1, tiled=True)
    mlp_got = seq_exchange(tie(mlp_send, modulation))
    mlp_shard, proj_shard = arrange(
        join_hidden,
        [((feat, 2 * ff_part), BF16), ((feat, proj_cols + 2 * zd_part), BF16)],
        mlp_got,
        third_proj,
    )
    mlp_all = lax.all_gather(mlp_shard, "img", axis=0, tiled=True)
    up_w, down_w = mlp_all[:, :ff_part], mlp_all[:, ff_part:]
    proj_all = lax.all_gather(proj_shard, "img", axis=0, tiled=True)
    proj_all = proj_all.reshape((img,) + proj_shard.shape)

    order = jnp.arange(SEQ, dtype=jnp.int32)
    all_slots = slot_ids.reshape(SEQ, own_rows)[:, 0]
    ours = (place ^ order)[:, None] == order[None, :]
    block_slots = jnp.sum(jnp.where(ours, all_slots[None, :], 0), axis=1)
    block_mod = sum(
        jnp.where((block_slots == slot)[:, None], modulation[slot][None, :], 0.0)
        for slot in range(slot_count)
    )
    shift_a, scale_a, gate_a, shift_b, scale_b, gate_b = jnp.split(block_mod[0], 6)

    def modulated(rows, first):
        normed, _ = norm_parts(rows.astype(F32).reshape(2, own_rows, width))
        shift = block_mod[first : first + 2, None, :width]
        scale = block_mod[first : first + 2, None, width : 2 * width]
        return (normed * (1.0 + scale) + shift).astype(BF16).reshape(2 * own_rows, width)

    hidden_a = jnp.concatenate([modulated(rows_full[0], 0), modulated(rows_full[1], 2)], 0)

    def open_attn(block, attn_ref):
        attn_ref[...] = block[...]

    def all_seq(part):
        across = swap(part, 2)
        return [part, swap(part, 1), across, swap(across, 1)]

    attn_part = open_spread(open_attn, [attn_weight.shape], swaps, swap_where)[0]
    attn_blocks = all_seq(attn_part)
    attn_w = join_columns(attn_blocks, place).reshape(width, width)
    zeros = jnp.zeros_like(query_bias)
    qkv_bias = jnp.concatenate([query_bias, zeros, value_bias])
    qkv_bias = lax.dynamic_slice_in_dim(qkv_bias, place * 3 * part_width, 3 * part_width, 0)
    qkv_own = (product(hidden_a, qkv_w) + qkv_bias).astype(BF16)

    distance = place ^ order
    chunk = (SEQ, own_rows, part_width)
    wide = (own_rows, SEQ * part_width)

    def cut_three(where, ins, outs):
        for turn in range(SEQ):

            def put():
                for p in range(SEQ):
                    rows = slice(p * own_rows, (p + 1) * own_rows)
                    at = (turn ^ p) * part_width
                    for j in range(3):
                        piece = ins[0][rows, j * part_width : (j + 1) * part_width]
                        outs[j][:, at : at + part_width] = piece

            pl.when(where[0] == turn)(put)

    turns = [[(i, (3 * i + j) % SEQ) for i in range(SEQ)] for j in range(3)]
    three = arrange(cut_three, [(wide, BF16)] * 3, qkv_own, place=place)
    three = [tie(lax.ppermute(three[j], "seq", turns[j]), *swaps) for j in range(3)]

    def join_three(where, ins, outs):
        for turn in range(3):

            def put():
                for kind in range(3):
                    at = kind * part_width
                    for b in range(SEQ):
                        piece = ins[(kind + turn) % 3][:, b * part_width : (b + 1) * part_width]
                        outs[0][b, :, at : at + part_width] = piece

            pl.when(where[0] == turn)(put)

    joined = (SEQ, own_rows, 3 * part_width)
    qkv = arrange(join_three, [(joined, BF16)], *three, place=place % 3)[0]
    qkv = qkv.reshape(SEQ * own_rows, 3 * part_width)
    attended_h = attend_forward(qkv, all_slots)

    def by_distance_rows(where, ins, outs):
        for p in range(SEQ):
            outs[p][...] = ins[0][where[p]]

    attended_h = arrange(
        by_distance_rows,
        [((own_rows, part_width), BF16)] * SEQ,
        attended_h.reshape(chunk),
        place=distance,
    )
    heads_rel = [attended_h[0]] + [swap(attended_h[p], p) for p in range(1, SEQ)]
    attended = join_columns([tie(block, attn_w) for block in heads_rel], place)
    tokens_f = tokens.astype(F32)
    branch_a = product(attended, attn_w) + attn_bias
    after_attn = tokens_f + gate_a * branch_a
    normed_b, inverse_b = norm_parts(after_attn)
    hidden_b = gather_rows((normed_b * (1.0 + scale_b) + shift_b).astype(BF16))

    my_up_bias = up_bias.reshape(img, SEQ, ff_cell)
    my_up_bias = lax.dynamic_index_in_dim(my_up_bias, place, 1, keepdims=False).reshape(ff_part)

    def open_projector(ref, first_ref, second_ref, third_ref):
        first_ref[...] = ref[:, :ph_part]
        for side in range(2):
            rows = slice(side * ph_cell, (side + 1) * ph_cell)
            for d in range(SEQ):
                at, to = ph_part + d * half, (2 * d + side) * half
                second_ref[:, to : to + half] = ref[rows, at : at + half]
            at = proj_cols + side * zd_part
            rows = slice(side * third_rows, (side + 1) * third_rows)
            third_ref[rows, :] = ref[:third_rows, at : at + zd_part]

    first_w, second_w, third_part = open_blocks(
        open_projector, [(feat, ph_part), (ph_cell, ph), (2 * third_rows, zd_part)], proj_all
    )
    first_w, second_w = first_w.reshape(width, ph_part), second_w.reshape(ph_part, ph)
    third_w = jnp.concatenate(all_seq(third_part.reshape(ph, zd_part).T), 0)
    acts, slopes, sums = [], [], []
    for side in range(2):
        value, slope = gelu_parts(product(hidden_b[side], up_w) + my_up_bias)
        acts.append(value.astype(BF16))
        slopes.append(slope)
        sums.append(product(acts[side], down_w, BF16))
    branch_b = scatter_rows(*sums) + down_bias
    result = after_attn + gate_b * branch_b
    feed_low = result.astype(BF16)

    feed = gather_rows(feed_low)
    my_first_bias = first_bias.reshape(img, SEQ, ph_cell)
    my_first_bias = lax.dynamic_index_in_dim(my_first_bias, place, 1, keepdims=False)
    my_first_bias = my_first_bias.reshape(ph_part)
    first_acts, first_slopes, sums = [], [], []
    for side in range(2):
        value, slope = silu_parts(product(feed[side], first_w) + my_first_bias)
        first_acts.append(value.astype(BF16))
        first_slopes.append(slope)
        sums.append(product(first_acts[side], second_w, BF16))
    second_act, second_slope = silu_parts(scatter_rows(*sums) + second_bias)
    second_low = second_act.astype(BF16)
    def by_distance(values):
        blocks = values.reshape(values.shape[:-1] + (SEQ, zd_part))
        blocks = [
            lax.dynamic_index_in_dim(blocks, place ^ p, blocks.ndim - 2, keepdims=False)
            for p in range(SEQ)
        ]
        return jnp.concatenate(blocks, axis=-1)

    aligned = product_nt(second_low, third_w) + by_distance(third_bias)
    target = join_columns(split_columns(dino_target, place)).astype(F32)
    inv_z = lax.rsqrt(jnp.sum(aligned * aligned, axis=1, keepdims=True) + EPS_COS)
    inv_t = lax.rsqrt(jnp.sum(target * target, axis=1, keepdims=True) + EPS_COS)
    cosine = jnp.sum(aligned * target, axis=1, keepdims=True) * inv_z * inv_t
    grad_aligned = -LAMBDA_ALIGN * (target * inv_t - cosine * aligned * inv_z) * inv_z
    grad_aligned = grad_aligned.astype(BF16)

    grad_second = (product(grad_aligned, third_w) * second_slope).astype(BF16)
    third_blocks = [
        product_tn(second_low, grad_aligned[:, p * zd_part : (p + 1) * zd_part], BF16)
        for p in range(SEQ)
    ]
    grad_seconds = gather_rows(grad_second)
    third_sum = scatter_blocks(third_blocks, grad_seconds[1]).astype(BF16)
    grad_firsts, sums = [], []
    for side in range(2):
        rows = grad_seconds[side] if side == 0 else tie(grad_seconds[1], sums[0], *third_blocks)
        grad = product_nt(rows, second_w) * first_slopes[side]
        grad_firsts.append(grad.astype(BF16))
        sums.append(product_nt(grad_firsts[side], first_w, BF16))
    first_acts = tie(jnp.concatenate(first_acts, 0), sums[1], third_sum)
    second_term = product_tn(first_acts, jnp.concatenate(grad_seconds, 0), BF16)
    second_blocks = second_term.reshape(img, ph_cell, ph)
    second_half = pair_send(second_blocks)
    grad_first = jnp.concatenate(grad_firsts, 0)
    first_term = product_tn(tie(jnp.concatenate(feed, 0), sums[1]), grad_first, BF16)
    first_got = img_exchange(first_term.reshape(img, feat, ph_part))
    grad_result = tie(scatter_rows(*sums), second_term, first_term)
    grad_result = out_cotangent.astype(F32) + grad_result

    grad_branch_b = (gate_b * grad_result).astype(BF16)
    grad_branches = gather_rows(grad_branch_b)

    def pack_third(where, ins, outs):
        for i in range(img):
            for side in range(2):
                first = (2 * i + side) * third_rows
                at = side * zd_part
                outs[0][i, :third_rows, at : at + zd_part] = ins[0][first : first + third_rows]

    third_shape = (img, feat, 2 * zd_part)
    third_blocks = arrange(pack_third, [(third_shape, BF16)], third_sum)[0]
    third_half = pair_send(third_blocks)
    grad_pres, sums = [], []
    for side in range(2):
        rows = grad_branches[side] if side == 0 else tie(grad_branches[1], sums[0], first_got)
        grad = product_nt(rows, down_w) * slopes[side]
        grad_pres.append(grad.astype(BF16))
        sums.append(product_nt(grad_pres[side], up_w, BF16))
    acts = tie(jnp.concatenate(acts, 0), sums[1])
    down_term = product_tn(acts, jnp.concatenate(grad_branches, 0), BF16)
    down_sum = lax.psum_scatter(down_term, "img", scatter_dimension=0, tiled=True)
    grad_pre = jnp.concatenate(grad_pres, 0)
    up_term = product_tn(tie(jnp.concatenate(hidden_b, 0), sums[1]), grad_pre, BF16)
    up_blocks = up_term.reshape(img, feat, ff_part)
    up_half = pair_send(up_blocks)
    second_pair = pair_sum([second_blocks], [tie(second_half, grad_branches[1])])
    second_got = slow_exchange(tie(second_pair, first_got))
    grad_hidden_b = tie(scatter_rows(*sums), down_term, up_term, second_pair)
    grad_after = grad_result + norm_back(normed_b, inverse_b, grad_hidden_b * (1.0 + scale_b))

    grad_branch_a = (gate_a * grad_after).astype(BF16)
    grad_attended = product_nt(grad_branch_a, attn_w, BF16)
    grad_parts = split_columns(grad_attended, place)
    grad_heads = [grad_parts[0]] + [swap(grad_parts[p], p) for p in range(1, SEQ)]
    branch_cols = split_columns(grad_branch_a, place)
    attended = tie(attended, *grad_parts)
    attn_sum = scatter_blocks(
        [product_tn(attended, cols, BF16) for cols in branch_cols]
    ).astype(BF16)
    attn_sum = attn_sum.reshape(img, feat, part_width)
    attn_half = pair_send(attn_sum)
    up_pair = pair_sum([up_blocks, third_blocks], [tie(up_half, *grad_parts), third_half])
    up_got = slow_exchange(tie(up_pair, second_got))

    def rows_in_order(where, ins, outs):
        for p in range(SEQ):
            outs[0][where[p]] = ins[p][...]

    grad_heads = arrange(rows_in_order, [(chunk, BF16)], *grad_heads, place=distance)[0]
    grad_heads = grad_heads.reshape(SEQ * own_rows, part_width)
    grad_joined = attend_backward(qkv, grad_heads, all_slots)
    grad_joined = tie(grad_joined, attn_sum).reshape(joined)

    def cut_back(where, ins, outs):
        for turn in range(3):

            def put():
                for kind in range(3):
                    at = kind * part_width
                    for b in range(SEQ):
                        piece = ins[0][b, :, at : at + part_width]
                        outs[(kind + turn) % 3][:, b * part_width : (b + 1) * part_width] = piece

            pl.when(where[0] == turn)(put)

    backs = arrange(cut_back, [(wide, BF16)] * 3, grad_joined, place=place % 3)
    backs = [lax.ppermute(backs[j], "seq", [(b, a) for a, b in turns[j]]) for j in range(3)]
    backs = [tie(back, up_got) for back in backs]

    def join_back(where, ins, outs):
        for turn in range(SEQ):

            def put():
                for p in range(SEQ):
                    rows = slice(p * own_rows, (p + 1) * own_rows)
                    at = (turn ^ p) * part_width
                    for j in range(3):
                        piece = ins[j][:, at : at + part_width]
                        outs[0][rows, j * part_width : (j + 1) * part_width] = piece

            pl.when(where[0] == turn)(put)

    grad_qkv = arrange(join_back, [(qkv_own.shape, BF16)], *backs, place=place)[0]
    far = product_nt(grad_qkv[2 * own_rows :], qkv_w, BF16)
    qkv_term = product_tn(tie(hidden_a, far), grad_qkv, BF16)
    near = product_nt(tie(grad_qkv, qkv_term)[: 2 * own_rows], qkv_w, BF16)
    grad_hidden_a = scatter_rows(near, far)
    qkv_blocks = qkv_term.reshape(img, feat, 3 * part_width)
    normed_a, inverse_a = norm_parts(tokens_f)
    tokens_grad = grad_after + norm_back(normed_a, inverse_a, grad_hidden_a * (1.0 + scale_a))

    own_sums = jnp.concatenate(
        [
            column_sums(grad_hidden_a),
            column_sums(grad_hidden_a * normed_a),
            column_sums(grad_after * branch_a),
            column_sums(grad_hidden_b),
            column_sums(grad_hidden_b * normed_b),
            column_sums(grad_result * branch_b),
        ]
    )
    aligned_sums = column_sums(grad_aligned).reshape(SEQ, zd_part)
    by_place = [
        own_sums.reshape(SEQ, mod_cols),
        column_sums(grad_branch_a).reshape(SEQ, part_width),
        column_sums(grad_branch_b).reshape(SEQ, part_width),
        column_sums(grad_second).reshape(SEQ, ph_part),
        jnp.stack([pick(aligned_sums, place ^ j) for j in range(SEQ)]),
    ]
    by_place = jnp.concatenate(by_place, axis=1)
    seq_got = seq_exchange(by_place)
    qkv_half = tie(pair_send(qkv_blocks), seq_got)
    qkv_pair = pair_sum([qkv_blocks, attn_sum], [qkv_half, attn_half])
    member = (all_slots[None, :] == jnp.arange(slot_count, dtype=jnp.int32)[:, None]).astype(F32)
    grad_mod = jnp.sum(member[:, :, None] * seq_got[None, :, :mod_cols], axis=1)
    row_biases = jnp.sum(seq_got[:, mod_cols:], axis=0)
    bias_sums = jnp.concatenate(
        [
            row_biases,
            column_sums(grad_qkv),
            column_sums(grad_pre),
            column_sums(grad_first),
        ]
    )
    mod_size = slot_count * mod_cols
    leading = lax.reduce_precision(bias_sums, 8, 7)
    rest = bias_sums - leading
    packed = [grad_mod.reshape(mod_size), leading, rest]
    img_got = img_gather(jnp.concatenate([part.astype(BF16) for part in packed]))
    grad_mods = img_got[:, :mod_size].reshape(img * slot_count, mod_cols)
    bias_pairs = img_got[:, mod_size:].astype(F32).reshape(img * 2, bias_sums.shape[0])
    bias_sums = jnp.sum(bias_pairs, axis=0)
    ada_weight_grad = product_tn(cond_cols, grad_mods)
    cond_parts = product_nt(grad_mods, ada_weight).reshape(img, slot_count, feat)
    cond_parts = img_exchange(cond_parts).transpose(1, 0, 2).reshape(slot_count * width)
    def split_sums(where, ins, outs):
        for d in range(SEQ):
            at = d * part_width
            total = ins[0][0, :, at : at + part_width].astype(F32)
            for k in range(1, img // 2):
                total = total + ins[0][k, :, at : at + part_width].astype(F32)
            outs[0][d, :, :part_width] = total.astype(BF16)
            outs[0][d, :, part_width:first_at] = ins[1][:, at : at + part_width]
            at = d * first_width
            total = ins[2][0, :, at : at + first_width].astype(F32)
            for k in range(1, img):
                total = total + ins[2][k, :, at : at + first_width].astype(F32)
            outs[0][d, :, first_at:second_at] = total.astype(BF16)
            for side in range(2):
                rows = slice(side * ph_cell, (side + 1) * ph_cell)
                at = (2 * d + side) * half
                total = ins[3][0, :, at : at + half].astype(F32)
                for k in range(1, img // 2):
                    total = total + ins[3][k, :, at : at + half].astype(F32)
                outs[0][d, rows, second_at:] = total.astype(BF16)

    hidden_send = arrange(
        split_sums, [((SEQ, feat, hidden_cols), BF16)], tie(up_got, near), down_sum, first_got, second_got
    )[0]
    hidden_got = [swap(pick(hidden_send, place ^ p), p) for p in range(1, SEQ)]
    hidden_got = [pick(hidden_send, place)] + hidden_got

    def in_order(where, ins, outs):
        for p in range(SEQ):
            outs[0][where[p]] = ins[p][...]

    hidden_got = [tie(block, img_got) for block in hidden_got]
    hidden_got = arrange(in_order, [(hidden_send.shape, BF16)], *hidden_got, place=distance)[0]

    qkv_attn_grad = slow_scatter(qkv_pair, cond_parts)
    qkv_weight_grad = qkv_attn_grad[:, : 3 * part_width]
    attn_weight_grad = qkv_attn_grad[:, 3 * part_width :]
    last = jnp.concatenate([column_sums(grad_mods), bias_sums, cond_parts])
    last = jnp.pad(last, (0, -last.shape[0] % 1024))
    last = lax.all_gather(last, "seq", axis=0, tiled=False)
    sizes = [mod_cols, part_width, part_width, ph_part, zd // SEQ, 3 * part_width]
    sizes += [ff_part, ph_part, slot_count * width]
    cuts, start = [], 0
    for size in sizes:
        cuts.append(last[:, start : start + size])
        start += size
    ada_bias_grad, attn_bias_grad, down_bias_grad, second_bias_grad, third_bias_grad = (
        cut.reshape(-1) for cut in cuts[:5]
    )
    qkv_bias_grad = cuts[5].reshape(-1)
    query_bias_grad, value_bias_grad = qkv_bias_grad[:width], qkv_bias_grad[2 * width :]
    up_bias_grad = cuts[6].reshape(SEQ, img, ff_cell).transpose(1, 0, 2).reshape(ff)
    first_bias_grad = cuts[7].reshape(SEQ, img, ph_cell).transpose(1, 0, 2).reshape(ph)
    conditioning_grad = jnp.sum(cuts[8], axis=0).reshape(slot_count, width) * cond_slope

    def join_cells(where, ins, outs):
        up, down, first, second = outs
        for d in range(SEQ):
            part = ins[0].at[d]
            for j in range(cells):
                at = (j * SEQ + d) * ff_cell
                up[:, at : at + ff_cell] = part[:, j * ff_cell : (j + 1) * ff_cell].astype(F32)
                at, to = (j * SEQ + d) * ph_cell, first_at + j * ph_cell
                first[:, at : at + ph_cell] = part[:, to : to + ph_cell].astype(F32)
            down[d] = part[:, part_width:first_at].astype(F32)
            for side in range(2):
                rows = slice(side * ph_cell, (side + 1) * ph_cell)
                second[d, :, side * half : (side + 1) * half] = part[rows, second_at:].astype(F32)

    up_weight_grad, down_weight_grad, first_proj_grad, second_proj_grad = arrange(
        join_cells,
        [
            ((feat, ff_part), F32),
            ((SEQ, ff_cell, part_width), F32),
            ((feat, ph_part), F32),
            ((SEQ, ph_cell, ph_part), F32),
        ],
        hidden_got,
    )
    down_weight_grad = down_weight_grad.reshape(ff // img, part_width)
    second_proj_grad = second_proj_grad.reshape(ph // img, ph_part)

    def open_third(where, ins, outs):
        for side in range(2):
            at = ff_part + side * zd_part
            total = ins[0][0, :third_rows, at : at + zd_part].astype(F32)
            for k in range(1, img // 2):
                total = total + ins[0][k, :third_rows, at : at + zd_part].astype(F32)
            outs[0][side * third_rows : (side + 1) * third_rows] = total

    third_proj_grad = arrange(open_third, [(third_proj.shape, F32)], tie(up_got, img_got))[0]
    return (
        feed_low,
        tokens_grad,
        conditioning_grad,
        ada_weight_grad,
        qkv_weight_grad,
        attn_weight_grad,
        up_weight_grad,
        down_weight_grad,
        first_proj_grad,
        second_proj_grad,
        third_proj_grad,
        ada_bias_grad,
        query_bias_grad,
        value_bias_grad,
        attn_bias_grad,
        up_bias_grad,
        down_bias_grad,
        first_bias_grad,
        second_bias_grad,
        third_bias_grad,
    )


def solution(mesh):
    rows = P(("img", "seq"), None)
    both = P("img", "seq")
    return jax.shard_map(
        local,
        mesh=mesh,
        in_specs=(rows, P("img", None), P("img"), rows, rows) + (both,) * 8 + (P(),) * 9,
        out_specs=(rows, rows, P("img", None)) + (both,) * 8 + (P(),) * 9,
        check_vma=False,
    )
```
